512 devices in a mesh: row: 32 (over z, core), col: 16 (over y, x).
Axes of the slice: x: 4, y: 4, z: 16, core: 2. Of those that a mesh axis runs over, the one named last changes fastest.
Arguments:
- gbar: float32 [4, 4096, 8, 2048], P(None, 'row', None, 'col'), as said below
- panel: float32 [8, 2048, 256], P(None, ('col', 'row')), may hold values from -0.046875 to 0.046875
- panel_adj: float32 [4, 4096, 256], P(None, ('row', 'col')), may hold values from -6 to 6
- factor: float32 [256, 256], replicated, as said below
- factor_adj: float32 [256, 256], replicated, may hold values from -6 to 6
Outputs:
- lower_adj: float32 [4, 4096, 256], P(None, ('row', 'col'))
- corner_adj: float32 [256, 256], replicated
The draws below stay inside these ranges and needn't reach their ends.
Inputs may be any that keep to these rules, and one draw needn't show every extreme that they name: gbar holds a symmetric 16384 x 16384 matrix. factor is lower triangular with a positive diagonal.
All inputs are finite; a program needn't handle non-finite values.
Results may differ from the reference program's by a relative error of at most 0.000075.
Values sent between devices are 32-bit elements; how exact they have to be, the bound alone decides.
No kernel may reach another device: no remote copies, remote signals or barrier semaphores. Data moves between devices by JAX's collectives and lax.ppermute only.
A program may use at most 64 MiB of HBM per device.

```python
import jax
import jax.numpy as jnp
from jax import lax

N = 16384
B = 256
ROW_BLOCKS = 4
COL_BLOCKS = 8


def draw_gbar(key, part):
    first = jax.random.fold_in(key, 11)
    values = jax.random.normal(first, (N, N), jnp.float32)
    matrix = (values + values.T) * 0.35355339
    return matrix.reshape(ROW_BLOCKS, N // ROW_BLOCKS, COL_BLOCKS, N // COL_BLOCKS)


def draw_factor(key, part):
    first = jax.random.fold_in(key, 21)
    second = jax.random.fold_in(key, 22)
    diagonal = jax.random.uniform(first, (B,), jnp.float32, 1.5, 3.0)
    lower = jax.random.normal(second, (B, B), jnp.float32)
    lower = lower * (0.5 * B ** (-0.5))
    return jnp.tril(lower, -1) + jnp.diag(diagonal)


def levels(stream_key, shape, cuts, low, largest):
    gain = 1.0
    for position, blocks in cuts:
        draws = jax.random.uniform(jax.random.fold_in(jax.random.fold_in(stream_key, 6), position), (blocks,), jnp.float32, low / len(cuts), largest / len(cuts))
        gain = gain * jnp.repeat(jnp.exp(draws), shape[position] // blocks).reshape((-1,) + (1,) * (len(shape) - 1 - position))
    return gain


def centred(own_key, extent, scale, bound, shards=(), held_as=jnp.bfloat16):
    gain = levels(own_key, extent, shards, -0.22, 0.18) if shards else 1.0
    drawn = jax.random.normal(own_key, extent, jnp.float32) * scale * gain
    return jnp.minimum(jnp.maximum(drawn, -bound), bound).astype(held_as)


def setup_inputs(seed: int = 0) -> dict:
    streams_of = jax.random.split(jax.random.key(seed), 6)
    gbar = draw_gbar(jax.random.fold_in(streams_of[5], 71), 0)
    panel = centred(streams_of[1], (COL_BLOCKS, N // COL_BLOCKS, B), N ** -0.5, 0.046875, ((1, 512),), jnp.float32)
    panel_adj = centred(streams_of[2], (ROW_BLOCKS, N // ROW_BLOCKS, B), 1.0, 6.0, ((1, 512),), jnp.float32)
    factor = draw_factor(jax.random.fold_in(streams_of[5], 71), 0)
    factor_adj = centred(streams_of[4], (B, B), 1.0, 6.0, (), jnp.float32)
    return {"gbar": gbar, "panel": panel, "panel_adj": panel_adj, "factor": factor, "factor_adj": factor_adj}


def reference(gbar, panel, panel_adj, factor, factor_adj):
    highest = lax.Precision.HIGHEST
    matrix = gbar.reshape(N, N)
    columns = panel.reshape(N, B)
    adjoint = panel_adj.reshape(N, B)
    trailing = jnp.dot(matrix.astype(jnp.float32), columns.astype(jnp.float32), precision=highest, preferred_element_type=jnp.float32)
    panel_total = adjoint - 2.0 * trailing
    inverse = jax.scipy.linalg.solve_triangular(factor, jnp.eye(B, dtype=jnp.float32), lower=True)
    lower_full = jnp.dot(panel_total.astype(jnp.float32), inverse.astype(jnp.float32), precision=highest, preferred_element_type=jnp.float32)
    diag_total = factor_adj - jnp.dot(lower_full.T.astype(jnp.float32), columns.astype(jnp.float32), precision=highest, preferred_element_type=jnp.float32)
    projected = jnp.dot(factor.T.astype(jnp.float32), diag_total.astype(jnp.float32), precision=highest, preferred_element_type=jnp.float32)
    halved = jnp.tril(projected) - 0.5 * jnp.diag(jnp.diag(projected))
    middle = jnp.dot(jnp.dot(inverse.T.astype(jnp.float32), halved.astype(jnp.float32), precision=highest, preferred_element_type=jnp.float32).astype(jnp.float32), inverse.astype(jnp.float32), precision=highest, preferred_element_type=jnp.float32)
    corner_adj = 0.5 * (middle + middle.T)
    return (lower_full.reshape(panel_adj.shape), corner_adj)
```

```python
import jax
import jax.numpy as jnp
from jax import lax
from jax.sharding import Mesh
from jax.sharding import PartitionSpec as P


def dot(a, b):
    return jnp.dot(a, b, precision=lax.Precision.HIGHEST, preferred_element_type=jnp.float32)


def spread(block, axis):
    n = lax.axis_size(axis)
    return lax.all_to_all(jnp.broadcast_to(block[None], (n,) + block.shape), axis, 0, 0, tiled=True)


def per_device(gbar, panel, panel_adj, factor, factor_adj):
    highest = lax.Precision.HIGHEST
    core_at = lax.axis_index("core")
    row_at = lax.axis_index("z") * lax.axis_size("core") + core_at
    col_at = lax.axis_index("col")
    n_z = lax.axis_size("z")
    n_core = lax.axis_size("core")
    n_col = lax.axis_size("col")
    width = factor.shape[0]
    row_blocks, rows, col_blocks, cols = gbar.shape
    share = panel_adj.shape[1]
    part = panel.shape[1]
    own = panel.reshape(col_blocks * part, width)
    along_z = lax.all_gather(own, "z", axis=0)
    both = lax.all_gather(along_z, "core", axis=0)
    column = both.reshape(n_core, n_z, col_blocks, part, width).transpose(2, 1, 0, 3, 4)
    column = column.reshape(col_blocks, cols, width)
    product = jnp.einsum(
        "arcs,csk->ark", gbar, column, precision=highest, preferred_element_type=jnp.float32
    )
    inverse = jax.scipy.linalg.solve_triangular(
        factor, jnp.eye(width, dtype=jnp.float32), lower=True
    )
    ratio = col_blocks // row_blocks
    local = lax.dynamic_index_in_dim(
        column.reshape(row_blocks, ratio, cols, width), row_at // n_col, 1, keepdims=False
    )
    sent = jnp.stack([product, local])
    sent = sent.reshape(2, row_blocks, n_col, share, width).transpose(2, 0, 1, 3, 4)
    got = lax.all_to_all(sent, "col", 0, 0, tiled=True)
    total = panel_adj - 2.0 * jnp.sum(got[:, 0], axis=0)
    mine = lax.dynamic_index_in_dim(got[:, 1], row_at % n_col, 0, keepdims=False)
    total = total.reshape(row_blocks * share, width)
    mine = mine.reshape(row_blocks * share, width)
    lower = dot(total, inverse)
    corner = dot(mine.T, lower)
    slices = lax.all_to_all(corner.reshape(n_col, width // n_col, width), "col", 0, 0, tiled=True)
    slice_col = jnp.sum(slices, axis=0)
    half = width // n_col // n_core
    halves = lax.all_to_all(slice_col.reshape(n_core, half, width), "core", 0, 0, tiled=True)
    piece = jnp.sum(halves, axis=0)
    piece = jnp.sum(spread(piece, "z"), axis=0)
    begin = (col_at * n_core + core_at) * half
    adjusted = lax.dynamic_slice_in_dim(factor_adj.T, begin, half, 0) - piece
    projected = dot(adjusted, factor)
    at_row = begin + lax.broadcasted_iota(jnp.int32, projected.shape, 0)
    at_col = lax.broadcasted_iota(jnp.int32, projected.shape, 1)
    scale = jnp.where(at_row < at_col, 1.0, jnp.where(at_row == at_col, 0.5, 0.0))
    halved = jnp.where(at_row <= at_col, projected * scale, 0.0)
    stage = dot(halved, inverse)
    stage = lax.all_gather(stage, "core", axis=0, tiled=True)
    stage = spread(stage, "col").reshape(width, width)
    middle = dot(inverse.T, stage)
    return (lower.reshape(row_blocks, share, width), 0.5 * (middle + middle.T))


def solution(mesh):
    devices = mesh.devices
    wide = Mesh(devices.reshape(devices.shape[0] // 2, 2, devices.shape[1]), ("z", "core", "col"))
    row = ("z", "core")
    return jax.shard_map(
        per_device,
        mesh=wide,
        in_specs=(
            P(None, row, None, "col"),
            P(None, ("col",) + row, None),
            P(None, row + ("col",), None),
            P(),
            P(),
        ),
        out_specs=(P(None, row + ("col",), None), P()),
        check_vma=False,
    )
```

```python
import jax
import jax.numpy as jnp
from jax import lax
from jax.experimental import pallas as pl
from jax.experimental.pallas import tpu as pltpu
from jax.sharding import Mesh
from jax.sharding import PartitionSpec as P

HIGHEST = lax.Precision.HIGHEST
F32 = jnp.float32


def dot(a, b):
    return jnp.dot(a, b, precision=HIGHEST, preferred_element_type=F32)


def dot_tn(a, b):
    return lax.dot_general(
        a, b, (((0,), (0,)), ((), ())), precision=HIGHEST, preferred_element_type=F32
    )


def call(kernel, outs, *args, scratch=(), scalars=0, cost=None):
    specs = [pl.BlockSpec(memory_space=pltpu.SMEM)] * scalars
    specs += [pl.BlockSpec(memory_space=pltpu.VMEM)] * (len(args) - scalars)
    return pl.pallas_call(
        kernel,
        out_shape=jax.tree.map(lambda s: jax.ShapeDtypeStruct(s, F32), outs, is_leaf=lambda s: isinstance(s, tuple) and isinstance(s[0], int)),
        in_specs=specs,
        scratch_shapes=scratch,
        cost_estimate=cost,
        compiler_params=pltpu.CompilerParams(vmem_limit_bytes=32 << 20),
    )(*args)


def invert_kernel(factor_ref, out_ref):
    n = factor_ref.shape[0]
    i = lax.broadcasted_iota(jnp.int32, (n, n), 0)
    j = lax.broadcasted_iota(jnp.int32, (n, n), 1)
    lower = factor_ref[...]
    out_ref[...] = jnp.where(i == j, 1.0 / jnp.where(i == j, lower, 1.0), 0.0)
    size = 1
    while size < n:
        below = (i // size == j // size + 1) & (j // size % 2 == 0)
        now = out_ref[...]
        out_ref[...] = now - dot(dot(now, jnp.where(below, lower, 0.0)), now)
        size *= 2


def product_kernel(parity_ref, gbar_ref, both_ref, out_ref, column_ref):
    n_core, n_z, depth, width = both_ref.shape
    col_blocks = column_ref.shape[0]
    row_blocks = gbar_ref.shape[0]
    part = depth // col_blocks
    cols = gbar_ref.shape[2]
    rows = gbar_ref.shape[1] // col_blocks
    share = out_ref.shape[2] // row_blocks
    n_col = out_ref.shape[0]
    for c in range(col_blocks):
        for core in range(n_core):
            column_ref[c, :, core * part:(core + 1) * part, :] = both_ref[core, :, c * part:(c + 1) * part, :]
    full = column_ref[...].reshape(col_blocks * cols, width)
    for b in range(row_blocks):
        left = jnp.concatenate(
            [gbar_ref[b, pl.ds(c, rows, stride=col_blocks), :] for c in range(col_blocks)], axis=1
        )
        out_ref[:, 0, b * share:(b + 1) * share, :] = dot(left, full).reshape(n_col, share, width)
    ratio = col_blocks // row_blocks
    for b in range(row_blocks):
        local = column_ref[b * ratio + parity_ref[0]]
        out_ref[:, 1, b * share:(b + 1) * share, :] = local.reshape(n_col, share, width)


def owned_kernel(source_ref, got_ref, adjoint_ref, inverse_ref, lower_ref, corner_ref):
    n_col = got_ref.shape[0]
    total = got_ref[0, 0]
    for c in range(1, n_col):
        total = total + got_ref[c, 0]
    lower = dot(adjoint_ref[...] - 2.0 * total, inverse_ref[...])
    lower_ref[...] = lower
    corner_ref[...] = dot_tn(got_ref[source_ref[0], 1], lower).reshape(corner_ref.shape)


def fold_kernel(parts_ref, out_ref):
    total = jnp.sum(parts_ref[...], axis=0)
    out_ref[...] = jnp.broadcast_to(total[None], out_ref.shape)


def slice_kernel(begin_ref, parts_ref, adjoint_ref, factor_ref, inverse_ref, out_ref):
    count = out_ref.shape[1]
    begin = pl.multiple_of(begin_ref[0], count)
    adjusted = adjoint_ref[pl.ds(begin, count), :] - jnp.sum(parts_ref[...], axis=0)
    projected = dot(adjusted, factor_ref[...])
    at_row = begin + lax.broadcasted_iota(jnp.int32, projected.shape, 0)
    at_col = lax.broadcasted_iota(jnp.int32, projected.shape, 1)
    halved = jnp.where(at_row < at_col, projected, jnp.where(at_row == at_col, 0.5 * projected, 0.0))
    stage = dot(halved, inverse_ref[...])
    out_ref[...] = jnp.broadcast_to(stage[None], out_ref.shape)


def finish_kernel(stage_ref, inverse_ref, out_ref):
    middle = dot_tn(inverse_ref[...], stage_ref[...])
    out_ref[...] = 0.5 * (middle + middle.T)


def per_device(gbar, panel, panel_adj, factor, factor_adj):
    n_z, n_core, n_col = (lax.axis_size(a) for a in ("z", "core", "col"))
    core_at = lax.axis_index("core")
    col_at = lax.axis_index("col")
    row_at = lax.axis_index("z") * n_core + core_at
    width = factor.shape[0]
    row_blocks, rows, col_blocks, cols = gbar.shape
    share = panel_adj.shape[1]
    part = panel.shape[1]
    near = ("core", "col")
    n_near = n_core * n_col
    count = width // n_near
    own = panel.reshape(col_blocks * part, width)
    along_z = lax.all_gather(own, "z", axis=0)
    both = lax.all_to_all(
        jnp.broadcast_to(along_z[None], (n_core,) + along_z.shape), "core", 0, 0, tiled=True
    )
    sent = call(
        product_kernel,
        (n_col, 2, row_blocks * share, width),
        (row_at // n_col)[None],
        gbar.reshape(row_blocks, rows * col_blocks, cols),
        both,
        scratch=[pltpu.VMEM((col_blocks, n_z, n_core * part, width), F32)],
        scalars=1,
        cost=pl.CostEstimate(flops=int(1.6e9), bytes_accessed=4 << 20, transcendentals=0),
    )
    got = lax.all_to_all(sent, "col", 0, 0, tiled=True)
    inverse = call(
        invert_kernel,
        (width, width),
        factor,
        cost=pl.CostEstimate(flops=int(3.2e9), bytes_accessed=1 << 19, transcendentals=0),
    )
    lower, corner = call(
        owned_kernel,
        [(row_blocks * share, width), (n_near, count, width)],
        (row_at % n_col)[None],
        got,
        panel_adj.reshape(row_blocks * share, width),
        inverse,
        scalars=1,
    )
    slices = lax.all_to_all(corner, near, 0, 0, tiled=True)
    piece = lax.all_to_all(call(fold_kernel, (n_z, count, width), slices), "z", 0, 0, tiled=True)
    stage = call(
        slice_kernel,
        (n_near, count, width),
        ((core_at * n_col + col_at) * count)[None],
        piece,
        factor_adj.T,
        factor,
        inverse,
        scalars=1,
    )
    stage = lax.all_to_all(stage, near, 0, 0, tiled=True).reshape(width, width)
    corner_adj = call(finish_kernel, (width, width), stage, inverse)
    return lower.reshape(row_blocks, share, width), corner_adj


def solution(mesh):
    devices = mesh.devices
    wide = Mesh(devices.reshape(devices.shape[0] // 2, 2, devices.shape[1]), ("z", "core", "col"))
    row = ("z", "core")
    return jax.shard_map(
        per_device,
        mesh=wide,
        in_specs=(
            P(None, row, None, "col"),
            P(None, ("col",) + row, None),
            P(None, row + ("col",), None),
            P(),
            P(),
        ),
        out_specs=(P(None, row + ("col",), None), P()),
        check_vma=False,
    )
```

```python
import jax
import jax.numpy as jnp
from jax import lax
from jax.experimental import pallas as pl
from jax.experimental.pallas import tpu as pltpu
from jax.sharding import Mesh
from jax.sharding import PartitionSpec as P

HIGHEST = lax.Precision.HIGHEST
F32 = jnp.float32


def dot(a, b):
    return jnp.dot(a, b, precision=HIGHEST, preferred_element_type=F32)


def dot_tn(a, b):
    return lax.dot_general(
        a, b, (((0,), (0,)), ((), ())), precision=HIGHEST, preferred_element_type=F32
    )


def call(kernel, outs, *args, scratch=(), scalars=0, cost=None):
    specs = [pl.BlockSpec(memory_space=pltpu.SMEM)] * scalars
    specs += [pl.BlockSpec(memory_space=pltpu.VMEM)] * (len(args) - scalars)
    return pl.pallas_call(
        kernel,
        out_shape=jax.tree.map(lambda s: jax.ShapeDtypeStruct(s, F32), outs, is_leaf=lambda s: isinstance(s, tuple) and isinstance(s[0], int)),
        in_specs=specs,
        scratch_shapes=scratch,
        cost_estimate=cost,
        compiler_params=pltpu.CompilerParams(vmem_limit_bytes=32 << 20),
    )(*args)


def invert_kernel(factor_ref, out_ref):
    n = factor_ref.shape[0]
    i = lax.broadcasted_iota(jnp.int32, (n, n), 0)
    j = lax.broadcasted_iota(jnp.int32, (n, n), 1)
    lower = factor_ref[...]
    out_ref[...] = jnp.where(i == j, 1.0 / jnp.where(i == j, lower, 1.0), 0.0)
    size = 1
    while size < n:
        below = (i // size == j // size + 1) & (j // size % 2 == 0)
        now = out_ref[...]
        out_ref[...] = now - dot(dot(now, jnp.where(below, lower, 0.0)), now)
        size *= 2


def product_kernel(where_ref, gbar_ref, both_ref, out_ref, column_ref):
    n_core, _, _, depth, width = both_ref.shape
    col_blocks = column_ref.shape[0]
    row_blocks = gbar_ref.shape[0]
    part = depth // col_blocks
    cols = gbar_ref.shape[2]
    rows = gbar_ref.shape[1] // col_blocks
    share = out_ref.shape[2] // row_blocks
    n_col = out_ref.shape[0]
    for c in range(col_blocks):
        for flip in range(2):
            for core in range(n_core):
                held = both_ref[where_ref[1] ^ (flip ^ core), :, flip, c * part:(c + 1) * part, :]
                column_ref[c, :, flip, core * part:(core + 1) * part, :] = held
    full = column_ref[...].reshape(col_blocks * cols, width)
    for b in range(row_blocks):
        left = jnp.concatenate(
            [gbar_ref[b, pl.ds(c, rows, stride=col_blocks), :] for c in range(col_blocks)], axis=1
        )
        out_ref[:, 0, b * share:(b + 1) * share, :] = dot(left, full).reshape(n_col, share, width)
    ratio = col_blocks // row_blocks
    for b in range(row_blocks):
        local = column_ref[b * ratio + where_ref[0]]
        out_ref[:, 1, b * share:(b + 1) * share, :] = local.reshape(n_col, share, width)


def owned_kernel(source_ref, got_ref, adjoint_ref, total_ref, corner_ref):
    n_col = got_ref.shape[0]
    product = got_ref[0, 0]
    for c in range(1, n_col):
        product = product + got_ref[c, 0]
    total = adjoint_ref[...] - 2.0 * product
    total_ref[...] = total
    corner_ref[...] = dot_tn(got_ref[source_ref[0], 1], total).reshape(corner_ref.shape)


def lower_kernel(total_ref, inverse_ref, out_ref):
    out_ref[...] = dot(total_ref[...], inverse_ref[...])


def fold_kernel(parts_ref, out_ref):
    total = jnp.sum(parts_ref[...], axis=0)
    out_ref[...] = jnp.broadcast_to(total[None], out_ref.shape)


def slice_kernel(begin_ref, parts_ref, adjoint_ref, factor_ref, inverse_ref, out_ref):
    count = out_ref.shape[1]
    begin = pl.multiple_of(begin_ref[0], count)
    summed = dot(jnp.sum(parts_ref[...], axis=0), inverse_ref[...])
    adjusted = adjoint_ref[pl.ds(begin, count), :] - summed
    projected = dot(adjusted, factor_ref[...])
    at_row = begin + lax.broadcasted_iota(jnp.int32, projected.shape, 0)
    at_col = lax.broadcasted_iota(jnp.int32, projected.shape, 1)
    halved = jnp.where(at_row < at_col, projected, jnp.where(at_row == at_col, 0.5 * projected, 0.0))
    stage = dot(halved, inverse_ref[...])
    out_ref[...] = jnp.broadcast_to(stage[None], out_ref.shape)


def finish_kernel(stage_ref, inverse_ref, out_ref):
    middle = dot_tn(inverse_ref[...], stage_ref[...])
    out_ref[...] = 0.5 * (middle + middle.T)


def per_device(gbar, panel, panel_adj, factor, factor_adj):
    n_z, n_core, n_col = (lax.axis_size(a) for a in ("z", "core", "col"))
    core_at = lax.axis_index("core")
    col_at = lax.axis_index("col")
    row_at = lax.axis_index("z") * n_core + core_at
    width = factor.shape[0]
    row_blocks, rows, col_blocks, cols = gbar.shape
    share = panel_adj.shape[1]
    part = panel.shape[1]
    near = ("core", "col")
    n_near = n_core * n_col
    count = width // n_near
    own = panel.reshape(col_blocks * part, width)
    rings = [[2 * z + (z + start) % 2 for z in range(n_z)] for start in range(2)]
    along_z = lax.all_gather(own, ("z", "core"), axis=0, axis_index_groups=rings)
    both = lax.all_to_all(
        jnp.broadcast_to(along_z[None], (n_core,) + along_z.shape), "core", 0, 0, tiled=True
    )
    source = (row_at % n_col)[None]
    adjoint = panel_adj.reshape(row_blocks * share, width)
    both, source, adjoint = lax.optimization_barrier((both, source, adjoint))
    sent = call(
        product_kernel,
        (n_col, 2, row_blocks * share, width),
        jnp.stack([row_at // n_col, lax.axis_index("z") % 2]),
        gbar.reshape(row_blocks, rows * col_blocks, cols),
        both.reshape(n_core, n_z // 2, 2, col_blocks * part, width),
        scratch=[pltpu.VMEM((col_blocks, n_z // 2, 2, n_core * part, width), F32)],
        scalars=1,
        cost=pl.CostEstimate(flops=int(1.6e9), bytes_accessed=4 << 20, transcendentals=0),
    )
    got = lax.all_to_all(sent, "col", 0, 0, tiled=True)
    total, corner = call(
        owned_kernel,
        [(row_blocks * share, width), (n_near, count, width)],
        source,
        got,
        adjoint,
        scalars=1,
    )
    slices = lax.all_to_all(corner, near, 0, 0, tiled=True)
    folded, factor = lax.optimization_barrier(
        (call(fold_kernel, (n_z, count, width), slices), factor)
    )
    piece = lax.all_to_all(folded, "z", 0, 0, tiled=True)
    inverse = call(
        invert_kernel,
        (width, width),
        factor,
        cost=pl.CostEstimate(flops=int(3.2e9), bytes_accessed=1 << 19, transcendentals=0),
    )
    lower = call(lower_kernel, (row_blocks * share, width), total, inverse)
    stage = call(
        slice_kernel,
        (n_near, count, width),
        ((core_at * n_col + col_at) * count)[None],
        piece,
        factor_adj.T,
        factor,
        inverse,
        scalars=1,
    )
    stage = lax.all_to_all(stage, near, 0, 0, tiled=True).reshape(width, width)
    corner_adj = call(finish_kernel, (width, width), stage, inverse)
    return lower.reshape(row_blocks, share, width), corner_adj


def solution(mesh):
    devices = mesh.devices
    wide = Mesh(devices.reshape(devices.shape[0] // 2, 2, devices.shape[1]), ("z", "core", "col"))
    row = ("z", "core")
    return jax.shard_map(
        per_device,
        mesh=wide,
        in_specs=(
            P(None, row, None, "col"),
            P(None, ("col",) + row, None),
            P(None, row + ("col",), None),
            P(),
            P(),
        ),
        out_specs=(P(None, row + ("col",), None), P()),
        check_vma=False,
    )
```

```python
import jax
import jax.numpy as jnp
from jax import lax
from jax.experimental import pallas as pl
from jax.experimental.pallas import tpu as pltpu
from jax.sharding import Mesh
from jax.sharding import PartitionSpec as P

HIGHEST = lax.Precision.HIGHEST
F32 = jnp.float32


def dot(a, b):
    return jnp.dot(a, b, precision=HIGHEST, preferred_element_type=F32)


def dot_tn(a, b):
    return lax.dot_general(
        a, b, (((0,), (0,)), ((), ())), precision=HIGHEST, preferred_element_type=F32
    )


def call(kernel, outs, *args, scratch=(), scalars=0, cost=None):
    specs = [pl.BlockSpec(memory_space=pltpu.SMEM)] * scalars
    specs += [pl.BlockSpec(memory_space=pltpu.VMEM)] * (len(args) - scalars)
    return pl.pallas_call(
        kernel,
        out_shape=jax.tree.map(lambda s: jax.ShapeDtypeStruct(s, F32), outs, is_leaf=lambda s: isinstance(s, tuple) and isinstance(s[0], int)),
        in_specs=specs,
        scratch_shapes=scratch,
        cost_estimate=cost,
        compiler_params=pltpu.CompilerParams(vmem_limit_bytes=32 << 20),
    )(*args)


def invert_kernel(factor_ref, out_ref):
    n = factor_ref.shape[0]
    i = lax.broadcasted_iota(jnp.int32, (n, n), 0)
    j = lax.broadcasted_iota(jnp.int32, (n, n), 1)
    lower = factor_ref[...]
    out_ref[...] = jnp.where(i == j, 1.0 / jnp.where(i == j, lower, 1.0), 0.0)
    size = 1
    while size < n:
        below = (i // size == j // size + 1) & (j // size % 2 == 0)
        now = out_ref[...]
        out_ref[...] = now - dot(dot(now, jnp.where(below, lower, 0.0)), now)
        size *= 2


def product_kernel(parity_ref, turn_ref, gbar_ref, first_ref, second_ref, out_ref, column_ref):
    n_core, pairs, _, _, part, width = first_ref.shape
    col_blocks = column_ref.shape[0]
    row_blocks = gbar_ref.shape[0]
    cols = gbar_ref.shape[2]
    rows = gbar_ref.shape[1] // col_blocks
    share = out_ref.shape[2] // row_blocks
    n_col = out_ref.shape[0]
    for c in range(col_blocks):
        for flip in range(2):
            for core in range(n_core):
                for at, from_ref in ((0, first_ref), (pairs, second_ref)):
                    held = from_ref[turn_ref[0] ^ (flip ^ core), :, flip, c]
                    column_ref[c, at:at + pairs, flip, core * part:(core + 1) * part, :] = held
    full = column_ref[...].reshape(col_blocks * cols, width)
    for b in range(row_blocks):
        left = jnp.concatenate(
            [gbar_ref[b, pl.ds(c, rows, stride=col_blocks), :] for c in range(col_blocks)], axis=1
        )
        out_ref[:, 0, b * share:(b + 1) * share, :] = dot(left, full).reshape(n_col, share, width)
    ratio = col_blocks // row_blocks
    for b in range(row_blocks):
        local = column_ref[b * ratio + parity_ref[0]]
        out_ref[:, 1, b * share:(b + 1) * share, :] = local.reshape(n_col, share, width)


def owned_kernel(source_ref, got_ref, adjoint_ref, total_ref, corner_ref):
    n_col = got_ref.shape[0]
    product = got_ref[0, 0]
    for c in range(1, n_col):
        product = product + got_ref[c, 0]
    total = adjoint_ref[...] - 2.0 * product
    total_ref[...] = total
    corner_ref[...] = dot_tn(got_ref[source_ref[0], 1], total).reshape(corner_ref.shape)


def lower_kernel(total_ref, inverse_ref, adjoint_ref, factor_ref, out_ref, known_ref):
    out_ref[...] = dot(total_ref[...], inverse_ref[...])
    known_ref[...] = dot_tn(adjoint_ref[...], factor_ref[...])


def fold_kernel(parts_ref, out_ref):
    total = jnp.sum(parts_ref[...], axis=0)
    out_ref[...] = jnp.broadcast_to(total[None], out_ref.shape)


def slice_kernel(begin_ref, parts_ref, known_ref, inverse_ref, out_ref):
    count = out_ref.shape[1]
    begin = pl.multiple_of(begin_ref[0], count)
    projected = known_ref[pl.ds(begin, count), :] - jnp.sum(parts_ref[...], axis=0)
    at_row = begin + lax.broadcasted_iota(jnp.int32, projected.shape, 0)
    at_col = lax.broadcasted_iota(jnp.int32, projected.shape, 1)
    halved = jnp.where(at_row < at_col, projected, jnp.where(at_row == at_col, 0.5 * projected, 0.0))
    stage = dot(halved, inverse_ref[...])
    out_ref[...] = jnp.broadcast_to(stage[None], out_ref.shape)


def finish_kernel(stage_ref, inverse_ref, out_ref):
    middle = dot_tn(inverse_ref[...], stage_ref[...])
    out_ref[...] = 0.5 * (middle + middle.T)


def per_device(gbar, panel, panel_adj, factor, factor_adj):
    n_z, n_core, n_col = (lax.axis_size(a) for a in ("z", "core", "col"))
    core_at = lax.axis_index("core")
    col_at = lax.axis_index("col")
    row_at = lax.axis_index("z") * n_core + core_at
    width = factor.shape[0]
    row_blocks, rows, col_blocks, cols = gbar.shape
    share = panel_adj.shape[1]
    part = panel.shape[1]
    near = ("core", "col")
    n_near = n_core * n_col
    count = width // n_near
    rings = [[2 * z + (z + start) % 2 for z in range(n_z)] for start in range(2)]
    along_z = lax.all_gather(panel, ("z", "core"), axis=0, axis_index_groups=rings, tiled=True)
    middle = n_z * col_blocks // 2
    first = lax.all_gather(along_z[:middle], "core", axis=0, tiled=True)
    rest, first = lax.optimization_barrier((along_z[middle:], first))
    both = [first, lax.all_gather(rest, "core", axis=0, tiled=True)]
    source = (row_at % n_col)[None]
    adjoint = panel_adj.reshape(row_blocks * share, width)
    *both, source, adjoint = lax.optimization_barrier((*both, source, adjoint))
    sent = call(
        product_kernel,
        (n_col, 2, row_blocks * share, width),
        (row_at // n_col)[None],
        (lax.axis_index("z") % 2)[None],
        gbar.reshape(row_blocks, rows * col_blocks, cols),
        *[b.reshape(n_core, n_z // 4, 2, col_blocks, part, width) for b in both],
        scratch=[pltpu.VMEM((col_blocks, n_z // 2, 2, n_core * part, width), F32)],
        scalars=2,
        cost=pl.CostEstimate(flops=int(1.6e9), bytes_accessed=4 << 20, transcendentals=0),
    )
    got = lax.all_to_all(sent, "col", 0, 0, tiled=True)
    total, corner = call(
        owned_kernel,
        [(row_blocks * share, width), (n_near, count, width)],
        source,
        got,
        adjoint,
        scalars=1,
    )
    slices = lax.all_to_all(corner, near, 0, 0, tiled=True)
    folded, factor = lax.optimization_barrier(
        (call(fold_kernel, (n_z, count, width), slices), factor)
    )
    piece = lax.all_to_all(folded, "z", 0, 0, tiled=True)
    inverse = call(
        invert_kernel,
        (width, width),
        factor,
        cost=pl.CostEstimate(flops=int(3.2e9), bytes_accessed=1 << 19, transcendentals=0),
    )
    lower, known = call(
        lower_kernel,
        [(row_blocks * share, width), (width, width)],
        total,
        inverse,
        factor_adj,
        factor,
    )
    stage = call(
        slice_kernel,
        (n_near, count, width),
        ((core_at * n_col + col_at) * count)[None],
        piece,
        known,
        inverse,
        scalars=1,
    )
    stage = lax.all_to_all(stage, near, 0, 0, tiled=True).reshape(width, width)
    corner_adj = call(finish_kernel, (width, width), stage, inverse)
    return lower.reshape(row_blocks, share, width), corner_adj


def solution(mesh):
    devices = mesh.devices
    wide = Mesh(devices.reshape(devices.shape[0] // 2, 2, devices.shape[1]), ("z", "core", "col"))
    row = ("z", "core")
    return jax.shard_map(
        per_device,
        mesh=wide,
        in_specs=(
            P(None, row, None, "col"),
            P(None, ("col",) + row, None),
            P(None, row + ("col",), None),
            P(),
            P(),
        ),
        out_specs=(P(None, row + ("col",), None), P()),
        check_vma=False,
    )
```

```python
import functools

import jax
import jax.numpy as jnp
from jax import lax
from jax.experimental import pallas as pl
from jax.experimental.pallas import tpu as pltpu
from jax.sharding import Mesh
from jax.sharding import PartitionSpec as P

HIGHEST = lax.Precision.HIGHEST
F32 = jnp.float32


def dot(a, b):
    return jnp.dot(a, b, precision=HIGHEST, preferred_element_type=F32)


def dot_tn(a, b):
    return lax.dot_general(
        a, b, (((0,), (0,)), ((), ())), precision=HIGHEST, preferred_element_type=F32
    )


def call(kernel, outs, *args, scratch=(), scalars=0, cost=None):
    specs = [pl.BlockSpec(memory_space=pltpu.SMEM)] * scalars
    specs += [pl.BlockSpec(memory_space=pltpu.VMEM)] * (len(args) - scalars)
    return pl.pallas_call(
        kernel,
        out_shape=jax.tree.map(lambda s: jax.ShapeDtypeStruct(s, F32), outs, is_leaf=lambda s: isinstance(s, tuple) and isinstance(s[0], int)),
        in_specs=specs,
        scratch_shapes=scratch,
        cost_estimate=cost,
        compiler_params=pltpu.CompilerParams(vmem_limit_bytes=32 << 20),
    )(*args)


def invert_kernel(factor_ref, out_ref):
    n = factor_ref.shape[0]
    i = lax.broadcasted_iota(jnp.int32, (n, n), 0)
    j = lax.broadcasted_iota(jnp.int32, (n, n), 1)
    lower = factor_ref[...]
    out_ref[...] = jnp.where(i == j, 1.0 / jnp.where(i == j, lower, 1.0), 0.0)
    size = 1
    while size < n:
        below = (i // size == j // size + 1) & (j // size % 2 == 0)
        now = out_ref[...]
        out_ref[...] = now - dot(dot(now, jnp.where(below, lower, 0.0)), now)
        size *= 2


def product_kernel(parity_ref, turn_ref, core_ref, gbar_ref, first_ref, second_ref, out_ref, column_ref):
    n_core, pairs, _, _, part, width = first_ref.shape
    col_blocks = column_ref.shape[0]
    row_blocks = gbar_ref.shape[0]
    cols = gbar_ref.shape[2]
    rows = gbar_ref.shape[1] // col_blocks
    share = rows // out_ref.shape[0]
    n_col = out_ref.shape[0]
    for c in range(col_blocks):
        for flip in range(2):
            for core in range(n_core):
                for at, from_ref in ((0, first_ref), (pairs, second_ref)):
                    held = from_ref[turn_ref[0] ^ (flip ^ core), :, flip, c]
                    column_ref[c, at:at + pairs, flip, core * part:(core + 1) * part, :] = held
    full = column_ref[...].reshape(col_blocks * cols, width)
    for b in range(row_blocks):
        left = jnp.concatenate(
            [gbar_ref[b, pl.ds(c, rows, stride=col_blocks), :] for c in range(col_blocks)], axis=1
        )
        out_ref[:, b * share:(b + 1) * share, :] = dot(left, full).reshape(n_col, share, width)
    ratio = col_blocks // row_blocks
    for b in range(row_blocks):
        local = column_ref[b * ratio + parity_ref[0]].reshape(n_col, share, width)
        at = row_blocks * share + b * part
        out_ref[:, at:at + part, :] = jnp.where(core_ref[0] == 0, local[:, :part], local[:, part:])


def owned_kernel(source_ref, got_ref, adjoint_ref, total_ref, halves_ref):
    owned = adjoint_ref.shape[0]
    total_ref[...] = adjoint_ref[...] - 2.0 * jnp.sum(got_ref[:, :owned, :], axis=0)
    for core in range(halves_ref.shape[0]):
        halves_ref[core] = got_ref[source_ref[0] + core, owned:, :]


def corner_kernel(part, core_ref, halves_ref, total_ref, corner_ref, mine_ref):
    n_core, _, half, _ = halves_ref.shape
    for core in range(n_core):
        rows = halves_ref[core, core_ref[0]]
        for b in range(half // part):
            at = (b * n_core + core) * part
            mine_ref[at:at + part, :] = rows[b * part:(b + 1) * part]
    corner_ref[...] = dot_tn(mine_ref[...], total_ref[...]).reshape(corner_ref.shape)


def lower_kernel(total_ref, inverse_ref, adjoint_ref, factor_ref, out_ref, known_ref):
    out_ref[...] = dot(total_ref[...], inverse_ref[...])
    known_ref[...] = dot_tn(adjoint_ref[...], factor_ref[...])


def fold_kernel(parts_ref, out_ref):
    total = jnp.sum(parts_ref[...], axis=0)
    out_ref[...] = jnp.broadcast_to(total[None], out_ref.shape)


def slice_kernel(begin_ref, parts_ref, known_ref, inverse_ref, out_ref):
    count = out_ref.shape[1]
    begin = pl.multiple_of(begin_ref[0], count)
    projected = known_ref[pl.ds(begin, count), :] - jnp.sum(parts_ref[...], axis=0)
    at_row = begin + lax.broadcasted_iota(jnp.int32, projected.shape, 0)
    at_col = lax.broadcasted_iota(jnp.int32, projected.shape, 1)
    halved = jnp.where(at_row < at_col, projected, jnp.where(at_row == at_col, 0.5 * projected, 0.0))
    stage = dot(halved, inverse_ref[...])
    out_ref[...] = jnp.broadcast_to(stage[None], out_ref.shape)


def finish_kernel(stage_ref, inverse_ref, out_ref):
    middle = dot_tn(inverse_ref[...], stage_ref[...])
    out_ref[...] = 0.5 * (middle + middle.T)


def per_device(gbar, panel, panel_adj, factor, factor_adj):
    n_z, n_core, n_col = (lax.axis_size(a) for a in ("z", "core", "col"))
    core_at = lax.axis_index("core")
    col_at = lax.axis_index("col")
    row_at = lax.axis_index("z") * n_core + core_at
    width = factor.shape[0]
    row_blocks, rows, col_blocks, cols = gbar.shape
    share = panel_adj.shape[1]
    part = panel.shape[1]
    near = ("core", "col")
    n_near = n_core * n_col
    count = width // n_near
    rings = [[2 * z + (z + start) % 2 for z in range(n_z)] for start in range(2)]
    along_z = lax.all_gather(panel, ("z", "core"), axis=0, axis_index_groups=rings, tiled=True)
    middle = n_z * col_blocks // 2
    first = lax.all_gather(along_z[:middle], "core", axis=0, tiled=True)
    rest, first = lax.optimization_barrier((along_z[middle:], first))
    both = [first, lax.all_gather(rest, "core", axis=0, tiled=True)]
    source = (lax.axis_index("z") * n_core % n_col)[None]
    core = core_at[None]
    adjoint = panel_adj.reshape(row_blocks * share, width)
    *both, source, core, adjoint = lax.optimization_barrier((*both, source, core, adjoint))
    sent = call(
        product_kernel,
        (n_col, row_blocks * (share + part), width),
        (row_at // n_col)[None],
        (lax.axis_index("z") % 2)[None],
        core,
        gbar.reshape(row_blocks, rows * col_blocks, cols),
        *[b.reshape(n_core, n_z // 4, 2, col_blocks, part, width) for b in both],
        scratch=[pltpu.VMEM((col_blocks, n_z // 2, 2, n_core * part, width), F32)],
        scalars=3,
        cost=pl.CostEstimate(flops=int(1.6e9), bytes_accessed=4 << 20, transcendentals=0),
    )
    got = lax.all_to_all(sent, "col", 0, 0, tiled=True)
    total, halves = call(
        owned_kernel,
        [(row_blocks * share, width), (n_core, row_blocks * part, width)],
        source,
        got,
        adjoint,
        scalars=1,
    )
    corner = call(
        functools.partial(corner_kernel, part),
        (n_near, count, width),
        core,
        lax.all_gather(halves, "core", axis=0),
        total,
        scratch=[pltpu.VMEM((row_blocks * share, width), F32)],
        scalars=1,
    )
    slices = lax.all_to_all(corner, near, 0, 0, tiled=True)
    folded, factor = lax.optimization_barrier(
        (call(fold_kernel, (n_z, count, width), slices), factor)
    )
    piece = lax.all_to_all(folded, "z", 0, 0, tiled=True)
    inverse = call(
        invert_kernel,
        (width, width),
        factor,
        cost=pl.CostEstimate(flops=int(3.2e9), bytes_accessed=1 << 19, transcendentals=0),
    )
    lower, known = call(
        lower_kernel,
        [(row_blocks * share, width), (width, width)],
        total,
        inverse,
        factor_adj,
        factor,
    )
    stage = call(
        slice_kernel,
        (n_near, count, width),
        ((core_at * n_col + col_at) * count)[None],
        piece,
        known,
        inverse,
        scalars=1,
    )
    stage = lax.all_to_all(stage, near, 0, 0, tiled=True).reshape(width, width)
    corner_adj = call(finish_kernel, (width, width), stage, inverse)
    return lower.reshape(row_blocks, share, width), corner_adj


def solution(mesh):
    devices = mesh.devices
    wide = Mesh(devices.reshape(devices.shape[0] // 2, 2, devices.shape[1]), ("z", "core", "col"))
    row = ("z", "core")
    return jax.shard_map(
        per_device,
        mesh=wide,
        in_specs=(
            P(None, row, None, "col"),
            P(None, ("col",) + row, None),
            P(None, row + ("col",), None),
            P(),
            P(),
        ),
        out_specs=(P(None, row + ("col",), None), P()),
        check_vma=False,
    )
```

```python
import functools

import jax
import jax.numpy as jnp
from jax import lax
from jax.experimental import pallas as pl
from jax.experimental.pallas import tpu as pltpu
from jax.sharding import Mesh
from jax.sharding import PartitionSpec as P

HIGHEST = lax.Precision.HIGHEST
F32 = jnp.float32


def dot(a, b):
    return jnp.dot(a, b, precision=HIGHEST, preferred_element_type=F32)


def dot_tn(a, b):
    return lax.dot_general(
        a, b, (((0,), (0,)), ((), ())), precision=HIGHEST, preferred_element_type=F32
    )


def call(kernel, outs, *args, scratch=(), scalars=0, cost=None):
    specs = [pl.BlockSpec(memory_space=pltpu.SMEM)] * scalars
    specs += [pl.BlockSpec(memory_space=pltpu.VMEM)] * (len(args) - scalars)
    return pl.pallas_call(
        kernel,
        out_shape=jax.tree.map(lambda s: jax.ShapeDtypeStruct(s, F32), outs, is_leaf=lambda s: isinstance(s, tuple) and isinstance(s[0], int)),
        in_specs=specs,
        scratch_shapes=scratch,
        cost_estimate=cost,
        compiler_params=pltpu.CompilerParams(vmem_limit_bytes=32 << 20),
    )(*args)


def invert_kernel(factor_ref, out_ref):
    n = factor_ref.shape[0]
    i = lax.broadcasted_iota(jnp.int32, (n, n), 0)
    j = lax.broadcasted_iota(jnp.int32, (n, n), 1)
    lower = factor_ref[...]
    out_ref[...] = jnp.where(i == j, 1.0 / jnp.where(i == j, lower, 1.0), 0.0)
    size = 1
    while size < n:
        below = (i // size == j // size + 1) & (j // size % 2 == 0)
        now = out_ref[...]
        out_ref[...] = now - dot(dot(now, jnp.where(below, lower, 0.0)), now)
        size *= 2


def product_kernel(parity_ref, turn_ref, core_ref, gbar_ref, first_ref, second_ref, out_ref, column_ref):
    n_core, pairs, _, _, part, width = first_ref.shape
    col_blocks = column_ref.shape[0]
    row_blocks = gbar_ref.shape[0]
    cols = gbar_ref.shape[2]
    rows = gbar_ref.shape[1] // col_blocks
    share = rows // out_ref.shape[0]
    n_col = out_ref.shape[0]
    for c in range(col_blocks):
        for flip in range(2):
            for core in range(n_core):
                for at, from_ref in ((0, first_ref), (pairs, second_ref)):
                    held = from_ref[turn_ref[0] ^ (flip ^ core), :, flip, c]
                    column_ref[c, at:at + pairs, flip, core * part:(core + 1) * part, :] = held
    full = column_ref[...].reshape(col_blocks * cols, width)
    for b in range(row_blocks):
        left = jnp.concatenate(
            [gbar_ref[b, pl.ds(c, rows, stride=col_blocks), :] for c in range(col_blocks)], axis=1
        )
        out_ref[:, b * share:(b + 1) * share, :] = dot(left, full).reshape(n_col, share, width)
    ratio = col_blocks // row_blocks
    for b in range(row_blocks):
        local = column_ref[b * ratio + parity_ref[0]].reshape(n_col, share, width)
        at = row_blocks * share + b * part
        out_ref[:, at:at + part, :] = jnp.where(core_ref[0] == 0, local[:, :part], local[:, part:])


def owned_kernel(source_ref, got_ref, adjoint_ref, total_ref, halves_ref):
    owned = adjoint_ref.shape[0]
    total_ref[...] = adjoint_ref[...] - 2.0 * jnp.sum(got_ref[:, :owned, :], axis=0)
    for core in range(halves_ref.shape[0]):
        halves_ref[core] = got_ref[source_ref[0] + core, owned:, :]


def corner_kernel(part, core_ref, turn_ref, halves_ref, total_ref, corner_ref, mine_ref):
    n_core, _, half, _ = halves_ref.shape
    for core in range(n_core):
        rows = halves_ref[core, core_ref[0]]
        for b in range(half // part):
            at = (b * n_core + core) * part
            mine_ref[at:at + part, :] = rows[b * part:(b + 1) * part]
    corner = dot_tn(mine_ref[...], total_ref[...])
    n_col = corner_ref.shape[0] // n_core
    for core in range(n_core):
        held = corner[core * n_col * corner_ref.shape[1]:(core + 1) * n_col * corner_ref.shape[1]]
        at = (turn_ref[0] ^ core) * n_col
        corner_ref[pl.ds(at, n_col)] = held.reshape(n_col, *corner_ref.shape[1:])


def lower_kernel(total_ref, inverse_ref, adjoint_ref, factor_ref, out_ref, known_ref):
    out_ref[...] = dot(total_ref[...], inverse_ref[...])
    known_ref[...] = dot_tn(adjoint_ref[...], factor_ref[...])


def fold_kernel(parts_ref, out_ref):
    total = jnp.sum(parts_ref[...], axis=0)
    out_ref[...] = jnp.broadcast_to(total[None], out_ref.shape)


def slice_kernel(begin_ref, parts_ref, known_ref, inverse_ref, out_ref):
    count = out_ref.shape[1]
    begin = pl.multiple_of(begin_ref[0], count)
    projected = known_ref[pl.ds(begin, count), :] - jnp.sum(parts_ref[...], axis=0)
    at_row = begin + lax.broadcasted_iota(jnp.int32, projected.shape, 0)
    at_col = lax.broadcasted_iota(jnp.int32, projected.shape, 1)
    halved = jnp.where(at_row < at_col, projected, jnp.where(at_row == at_col, 0.5 * projected, 0.0))
    stage = dot(halved, inverse_ref[...])
    out_ref[...] = jnp.broadcast_to(stage[None], out_ref.shape)


def finish_kernel(turn_ref, stage_ref, inverse_ref, out_ref):
    stage = jnp.concatenate([stage_ref[turn_ref[0] ^ core] for core in range(2)], axis=0)
    middle = dot_tn(inverse_ref[...], stage)
    out_ref[...] = 0.5 * (middle + middle.T)


def per_device(gbar, panel, panel_adj, factor, factor_adj):
    n_z, n_core, n_col = (lax.axis_size(a) for a in ("z", "core", "col"))
    core_at = lax.axis_index("core")
    col_at = lax.axis_index("col")
    row_at = lax.axis_index("z") * n_core + core_at
    width = factor.shape[0]
    row_blocks, rows, col_blocks, cols = gbar.shape
    share = panel_adj.shape[1]
    part = panel.shape[1]
    near = ("core", "col")
    n_near = n_core * n_col
    count = width // n_near
    rings = [[2 * z + (z + start) % 2 for z in range(n_z)] for start in range(2)]
    along_z = lax.all_gather(panel, ("z", "core"), axis=0, axis_index_groups=rings, tiled=True)
    middle = n_z * col_blocks // 2
    first = lax.all_gather(along_z[:middle], "core", axis=0, tiled=True)
    rest, first = lax.optimization_barrier((along_z[middle:], first))
    both = [first, lax.all_gather(rest, "core", axis=0, tiled=True)]
    source = (lax.axis_index("z") * n_core % n_col)[None]
    core = core_at[None]
    turn = (lax.axis_index("z") % 2)[None]
    adjoint = panel_adj.reshape(row_blocks * share, width)
    *both, source, core, turn, adjoint = lax.optimization_barrier((*both, source, core, turn, adjoint))
    sent = call(
        product_kernel,
        (n_col, row_blocks * (share + part), width),
        (row_at // n_col)[None],
        turn,
        core,
        gbar.reshape(row_blocks, rows * col_blocks, cols),
        *[b.reshape(n_core, n_z // 4, 2, col_blocks, part, width) for b in both],
        scratch=[pltpu.VMEM((col_blocks, n_z // 2, 2, n_core * part, width), F32)],
        scalars=3,
        cost=pl.CostEstimate(flops=int(1.6e9), bytes_accessed=4 << 20, transcendentals=0),
    )
    got = lax.all_to_all(sent, "col", 0, 0, tiled=True)
    total, halves = call(
        owned_kernel,
        [(row_blocks * share, width), (n_core, row_blocks * part, width)],
        source,
        got,
        adjoint,
        scalars=1,
    )
    corner = call(
        functools.partial(corner_kernel, part),
        (n_near, count, width),
        core,
        turn,
        lax.all_gather(halves, "core", axis=0),
        total,
        scratch=[pltpu.VMEM((row_blocks * share, width), F32)],
        scalars=2,
    )
    slices = lax.all_to_all(corner, near, 0, 0, tiled=True)
    folded, factor = lax.optimization_barrier(
        (call(fold_kernel, (n_z, count, width), slices), factor)
    )
    piece = lax.all_to_all(folded, ("z", "core"), 0, 0, tiled=True, axis_index_groups=rings)
    inverse = call(
        invert_kernel,
        (width, width),
        factor,
        cost=pl.CostEstimate(flops=int(3.2e9), bytes_accessed=1 << 19, transcendentals=0),
    )
    lower, known = call(
        lower_kernel,
        [(row_blocks * share, width), (width, width)],
        total,
        inverse,
        factor_adj,
        factor,
    )
    stage = call(
        slice_kernel,
        (n_near, count, width),
        (((core_at ^ turn[0]) * n_col + col_at) * count)[None],
        piece,
        known,
        inverse,
        scalars=1,
    )
    stage = lax.all_to_all(stage, near, 0, 0, tiled=True)
    stage = stage.reshape(n_core, width // n_core, width)
    corner_adj = call(finish_kernel, (width, width), turn, stage, inverse, scalars=1)
    return lower.reshape(row_blocks, share, width), corner_adj


def solution(mesh):
    devices = mesh.devices
    wide = Mesh(devices.reshape(devices.shape[0] // 2, 2, devices.shape[1]), ("z", "core", "col"))
    row = ("z", "core")
    return jax.shard_map(
        per_device,
        mesh=wide,
        in_specs=(
            P(None, row, None, "col"),
            P(None, ("col",) + row, None),
            P(None, row + ("col",), None),
            P(),
            P(),
        ),
        out_specs=(P(None, row + ("col",), None), P()),
        check_vma=False,
    )
```

```python
import functools

import jax
import jax.numpy as jnp
from jax import lax
from jax.experimental import pallas as pl
from jax.experimental.pallas import tpu as pltpu
from jax.sharding import Mesh
from jax.sharding import PartitionSpec as P

HIGHEST = lax.Precision.HIGHEST
F32 = jnp.float32


def dot(a, b):
    return jnp.dot(a, b, precision=HIGHEST, preferred_element_type=F32)


def dot_tn(a, b):
    return lax.dot_general(
        a, b, (((0,), (0,)), ((), ())), precision=HIGHEST, preferred_element_type=F32
    )


def call(kernel, outs, *args, scratch=(), scalars=0, cost=None):
    specs = [pl.BlockSpec(memory_space=pltpu.SMEM)] * scalars
    specs += [pl.BlockSpec(memory_space=pltpu.VMEM)] * (len(args) - scalars)
    return pl.pallas_call(
        kernel,
        out_shape=jax.tree.map(lambda s: jax.ShapeDtypeStruct(s, F32), outs, is_leaf=lambda s: isinstance(s, tuple) and isinstance(s[0], int)),
        in_specs=specs,
        scratch_shapes=scratch,
        cost_estimate=cost,
        compiler_params=pltpu.CompilerParams(vmem_limit_bytes=32 << 20),
    )(*args)


def invert_kernel(factor_ref, out_ref):
    n = factor_ref.shape[0]
    i = lax.broadcasted_iota(jnp.int32, (n, n), 0)
    j = lax.broadcasted_iota(jnp.int32, (n, n), 1)
    lower = factor_ref[...]
    out_ref[...] = jnp.where(i == j, 1.0 / jnp.where(i == j, lower, 1.0), 0.0)
    size = 1
    while size < n:
        below = (i // size == j // size + 1) & (j // size % 2 == 0)
        now = out_ref[...]
        out_ref[...] = now - dot(dot(now, jnp.where(below, lower, 0.0)), now)
        size *= 2


def product_kernel(parity_ref, turn_ref, core_ref, gbar_ref, first_ref, second_ref, out_ref, column_ref):
    n_core, pairs, _, _, part, width = first_ref.shape
    col_blocks = column_ref.shape[0]
    row_blocks = gbar_ref.shape[0]
    cols = gbar_ref.shape[2]
    rows = gbar_ref.shape[1] // col_blocks
    share = rows // out_ref.shape[0]
    n_col = out_ref.shape[0]
    for c in range(col_blocks):
        for flip in range(2):
            for core in range(n_core):
                for at, from_ref in ((0, first_ref), (pairs, second_ref)):
                    held = from_ref[turn_ref[0] ^ (flip ^ core), :, flip, c]
                    column_ref[c, at:at + pairs, flip, core * part:(core + 1) * part, :] = held
    full = column_ref[...].reshape(col_blocks * cols, width)
    for b in range(row_blocks):
        left = jnp.concatenate(
            [gbar_ref[b, pl.ds(c, rows, stride=col_blocks), :] for c in range(col_blocks)], axis=1
        )
        out_ref[:, b * share:(b + 1) * share, :] = dot(left, full).reshape(n_col, share, width)
    ratio = col_blocks // row_blocks
    for b in range(row_blocks):
        local = column_ref[b * ratio + parity_ref[0]].reshape(n_col, share, width)
        at = row_blocks * share + b * part
        out_ref[:, at:at + part, :] = jnp.where(core_ref[0] == 0, local[:, :part], local[:, part:])


def owned_kernel(source_ref, got_ref, adjoint_ref, total_ref, halves_ref):
    owned = adjoint_ref.shape[0]
    total_ref[...] = adjoint_ref[...] - 2.0 * jnp.sum(got_ref[:, :owned, :], axis=0)
    for core in range(halves_ref.shape[0]):
        halves_ref[core] = got_ref[source_ref[0] + core, owned:, :]


def corner_kernel(part, core_ref, halves_ref, total_ref, corner_ref, mine_ref):
    n_core, _, half, _ = halves_ref.shape
    for core in range(n_core):
        rows = halves_ref[core, core_ref[0]]
        for b in range(half // part):
            at = (b * n_core + core) * part
            mine_ref[at:at + part, :] = rows[b * part:(b + 1) * part]
    corner_ref[...] = dot_tn(mine_ref[...], total_ref[...]).reshape(corner_ref.shape)


def lower_kernel(total_ref, inverse_ref, adjoint_ref, factor_ref, out_ref, known_ref):
    out_ref[...] = dot(total_ref[...], inverse_ref[...])
    known_ref[...] = dot_tn(adjoint_ref[...], factor_ref[...])


def fold_kernel(parts_ref, out_ref):
    total = jnp.sum(parts_ref[...], axis=0)
    out_ref[...] = jnp.broadcast_to(total[None], out_ref.shape)


def slice_kernel(begin_ref, parts_ref, known_ref, inverse_ref, out_ref):
    count = out_ref.shape[1]
    begin = pl.multiple_of(begin_ref[0], count)
    projected = known_ref[pl.ds(begin, count), :] - jnp.sum(parts_ref[...], axis=0)
    at_row = begin + lax.broadcasted_iota(jnp.int32, projected.shape, 0)
    at_col = lax.broadcasted_iota(jnp.int32, projected.shape, 1)
    halved = jnp.where(at_row < at_col, projected, jnp.where(at_row == at_col, 0.5 * projected, 0.0))
    stage = dot(halved, inverse_ref[...])
    out_ref[...] = jnp.broadcast_to(stage[None], out_ref.shape)


def finish_kernel(stage_ref, inverse_ref, out_ref):
    middle = dot_tn(inverse_ref[...], stage_ref[...])
    out_ref[...] = 0.5 * (middle + middle.T)


def per_device(gbar, panel, panel_adj, factor, factor_adj):
    n_z, n_core, n_col = (lax.axis_size(a) for a in ("z", "core", "col"))
    core_at = lax.axis_index("core")
    col_at = lax.axis_index("col")
    row_at = lax.axis_index("z") * n_core + core_at
    width = factor.shape[0]
    row_blocks, rows, col_blocks, cols = gbar.shape
    share = panel_adj.shape[1]
    part = panel.shape[1]
    near = ("core", "col")
    n_near = n_core * n_col
    count = width // n_near
    rings = [[2 * z + (z + start) % 2 for z in range(n_z)] for start in range(2)]
    along_z = lax.all_gather(panel, ("z", "core"), axis=0, axis_index_groups=rings, tiled=True)
    middle = n_z * col_blocks // 2
    first = lax.all_gather(along_z[:middle], "core", axis=0, tiled=True)
    rest, first = lax.optimization_barrier((along_z[middle:], first))
    both = [first, lax.all_gather(rest, "core", axis=0, tiled=True)]
    source = (lax.axis_index("z") * n_core % n_col)[None]
    core_here = core_at[None]
    adjoint = panel_adj.reshape(row_blocks * share, width)
    *both, source, core_here, adjoint = lax.optimization_barrier((*both, source, core_here, adjoint))
    sent = call(
        product_kernel,
        (n_col, row_blocks * (share + part), width),
        (row_at // n_col)[None],
        (lax.axis_index("z") % 2)[None],
        core_here,
        gbar.reshape(row_blocks, rows * col_blocks, cols),
        *[b.reshape(n_core, n_z // 4, 2, col_blocks, part, width) for b in both],
        scratch=[pltpu.VMEM((col_blocks, n_z // 2, 2, n_core * part, width), F32)],
        scalars=3,
        cost=pl.CostEstimate(flops=int(1.6e9), bytes_accessed=4 << 20, transcendentals=0),
    )
    got = lax.all_to_all(sent, "col", 0, 0, tiled=True)
    total, halves = call(
        owned_kernel,
        [(row_blocks * share, width), (n_core, row_blocks * part, width)],
        source,
        got,
        adjoint,
        scalars=1,
    )
    corner = call(
        functools.partial(corner_kernel, part),
        (n_near, count, width),
        core_here,
        lax.all_gather(halves, "core", axis=0),
        total,
        scratch=[pltpu.VMEM((row_blocks * share, width), F32)],
        scalars=1,
    )
    slices = lax.all_to_all(corner, near, 0, 0, tiled=True)
    folded, factor = lax.optimization_barrier(
        (call(fold_kernel, (n_z, count, width), slices), factor)
    )
    lines = [[(z + n_z // 2) % n_z * n_core + core for z in range(n_z)] for core in range(n_core)]
    piece = lax.all_to_all(folded, ("z", "core"), 0, 0, tiled=True, axis_index_groups=lines)
    inverse = call(
        invert_kernel,
        (width, width),
        factor,
        cost=pl.CostEstimate(flops=int(3.2e9), bytes_accessed=1 << 19, transcendentals=0),
    )
    lower, known = call(
        lower_kernel,
        [(row_blocks * share, width), (width, width)],
        total,
        inverse,
        factor_adj,
        factor,
    )
    stage = call(
        slice_kernel,
        (n_near, count, width),
        ((core_at * n_col + col_at) * count)[None],
        piece,
        known,
        inverse,
        scalars=1,
    )
    stage = lax.all_to_all(stage, near, 0, 0, tiled=True).reshape(width, width)
    corner_adj = call(finish_kernel, (width, width), stage, inverse)
    return lower.reshape(row_blocks, share, width), corner_adj


def solution(mesh):
    devices = mesh.devices
    wide = Mesh(devices.reshape(devices.shape[0] // 2, 2, devices.shape[1]), ("z", "core", "col"))
    row = ("z", "core")
    return jax.shard_map(
        per_device,
        mesh=wide,
        in_specs=(
            P(None, row, None, "col"),
            P(None, ("col",) + row, None),
            P(None, row + ("col",), None),
            P(),
            P(),
        ),
        out_specs=(P(None, row + ("col",), None), P()),
        check_vma=False,
    )
```

```python
import functools

import jax
import jax.numpy as jnp
from jax import lax
from jax.experimental import pallas as pl
from jax.experimental.pallas import tpu as pltpu
from jax.sharding import Mesh
from jax.sharding import PartitionSpec as P

HIGHEST = lax.Precision.HIGHEST
F32 = jnp.float32


def dot(a, b):
    return jnp.dot(a, b, precision=HIGHEST, preferred_element_type=F32)


def dot_tn(a, b):
    return lax.dot_general(
        a, b, (((0,), (0,)), ((), ())), precision=HIGHEST, preferred_element_type=F32
    )


def call(kernel, outs, *args, scratch=(), scalars=0, cost=None):
    specs = [pl.BlockSpec(memory_space=pltpu.SMEM)] * scalars
    specs += [pl.BlockSpec(memory_space=pltpu.VMEM)] * (len(args) - scalars)
    return pl.pallas_call(
        kernel,
        out_shape=jax.tree.map(lambda s: jax.ShapeDtypeStruct(s, F32), outs, is_leaf=lambda s: isinstance(s, tuple) and isinstance(s[0], int)),
        in_specs=specs,
        scratch_shapes=scratch,
        cost_estimate=cost,
        compiler_params=pltpu.CompilerParams(vmem_limit_bytes=32 << 20),
    )(*args)


def invert_kernel(factor_ref, adjoint_ref, out_ref, known_ref):
    n = factor_ref.shape[0] // 2
    i = lax.broadcasted_iota(jnp.int32, (n, n), 0)
    j = lax.broadcasted_iota(jnp.int32, (n, n), 1)
    lowers = [factor_ref[:n, :n], factor_ref[n:, n:]]
    now = []
    for lower in lowers:
        diagonal = jnp.where(i == j, 1.0 / jnp.where(i == j, lower, 1.0), 0.0)
        scaled = jnp.sum(diagonal, axis=1, keepdims=True) * lower * jnp.sum(diagonal, axis=0, keepdims=True)
        now.append(diagonal - jnp.where((i == j + 1) & (j % 2 == 0), scaled, 0.0))
    size = 2
    while size < n:
        below = (i // size == j // size + 1) & (j // size % 2 == 0)
        turned = [dot(x, jnp.where(below, lower, 0.0)) for x, lower in zip(now, lowers)]
        now = [x - dot(t, x) for x, t in zip(now, turned)]
        size *= 2
    out_ref[:n, :n] = now[0]
    out_ref[:n, n:] = jnp.zeros((n, n), F32)
    out_ref[n:, n:] = now[1]
    out_ref[n:, :n] = -dot(dot(now[1], factor_ref[n:, :n]), now[0])
    known_ref[...] = dot_tn(adjoint_ref[...], factor_ref[...])


def product_kernel(parity_ref, turn_ref, core_ref, gbar_ref, first_ref, second_ref, out_ref, column_ref):
    n_core, pairs, _, _, part, width = first_ref.shape
    col_blocks = column_ref.shape[0]
    row_blocks = gbar_ref.shape[0]
    cols = gbar_ref.shape[2]
    rows = gbar_ref.shape[1] // col_blocks
    share = rows // out_ref.shape[0]
    n_col = out_ref.shape[0]
    for c in range(col_blocks):
        for flip in range(2):
            for core in range(n_core):
                for at, from_ref in ((0, first_ref), (pairs, second_ref)):
                    held = from_ref[turn_ref[0] ^ (flip ^ core), :, flip, c]
                    column_ref[c, at:at + pairs, flip, core * part:(core + 1) * part, :] = held
    full = column_ref[...].reshape(col_blocks * cols, width)
    for b in range(row_blocks):
        left = jnp.concatenate(
            [gbar_ref[b, pl.ds(c, rows, stride=col_blocks), :] for c in range(col_blocks)], axis=1
        )
        out_ref[:, b * share:(b + 1) * share, :] = dot(left, full).reshape(n_col, share, width)
    ratio = col_blocks // row_blocks
    for b in range(row_blocks):
        local = column_ref[b * ratio + parity_ref[0]].reshape(n_col, share, width)
        at = row_blocks * share + b * part
        out_ref[:, at:at + part, :] = jnp.where(core_ref[0] == 0, local[:, :part], local[:, part:])


def owned_kernel(source_ref, got_ref, adjoint_ref, total_ref, halves_ref):
    owned = adjoint_ref.shape[0]
    total_ref[...] = adjoint_ref[...] - 2.0 * jnp.sum(got_ref[:, :owned, :], axis=0)
    for core in range(halves_ref.shape[0]):
        halves_ref[core] = got_ref[source_ref[0] + core, owned:, :]


def corner_kernel(part, core_ref, halves_ref, total_ref, corner_ref, mine_ref):
    n_core, _, half, _ = halves_ref.shape
    for core in range(n_core):
        rows = halves_ref[core, core_ref[0]]
        for b in range(half // part):
            at = (b * n_core + core) * part
            mine_ref[at:at + part, :] = rows[b * part:(b + 1) * part]
    corner_ref[...] = dot_tn(mine_ref[...], total_ref[...]).reshape(corner_ref.shape)


def lower_kernel(total_ref, inverse_ref, out_ref):
    out_ref[...] = dot(total_ref[...], inverse_ref[...])


def fold_kernel(parts_ref, out_ref):
    total = jnp.sum(parts_ref[...], axis=0)
    out_ref[...] = jnp.broadcast_to(total[None], out_ref.shape)


def slice_kernel(begin_ref, parts_ref, known_ref, inverse_ref, out_ref):
    count = out_ref.shape[1]
    begin = pl.multiple_of(begin_ref[0], count)
    projected = known_ref[pl.ds(begin, count), :] - jnp.sum(parts_ref[...], axis=0)
    at_row = begin + lax.broadcasted_iota(jnp.int32, projected.shape, 0)
    at_col = lax.broadcasted_iota(jnp.int32, projected.shape, 1)
    halved = jnp.where(at_row < at_col, projected, jnp.where(at_row == at_col, 0.5 * projected, 0.0))
    stage = dot(halved, inverse_ref[...])
    out_ref[...] = jnp.broadcast_to(stage[None], out_ref.shape)


def finish_kernel(stage_ref, inverse_ref, out_ref):
    middle = dot_tn(inverse_ref[...], stage_ref[...])
    out_ref[...] = 0.5 * (middle + middle.T)


def per_device(gbar, panel, panel_adj, factor, factor_adj):
    n_z, n_core, n_col = (lax.axis_size(a) for a in ("z", "core", "col"))
    core_at = lax.axis_index("core")
    col_at = lax.axis_index("col")
    row_at = lax.axis_index("z") * n_core + core_at
    width = factor.shape[0]
    row_blocks, rows, col_blocks, cols = gbar.shape
    share = panel_adj.shape[1]
    part = panel.shape[1]
    near = ("core", "col")
    n_near = n_core * n_col
    count = width // n_near
    rings = [[2 * z + (z + start) % 2 for z in range(n_z)] for start in range(2)]
    along_z = lax.all_gather(panel, ("z", "core"), axis=0, axis_index_groups=rings, tiled=True)
    middle = n_z * col_blocks // 2
    first = lax.all_gather(along_z[:middle], "core", axis=0, tiled=True)
    rest, first = lax.optimization_barrier((along_z[middle:], first))
    both = [first, lax.all_gather(rest, "core", axis=0, tiled=True)]
    source = (lax.axis_index("z") * n_core % n_col)[None]
    core_here = core_at[None]
    adjoint = panel_adj.reshape(row_blocks * share, width)
    *both, source, core_here, adjoint = lax.optimization_barrier((*both, source, core_here, adjoint))
    sent = call(
        product_kernel,
        (n_col, row_blocks * (share + part), width),
        (row_at // n_col)[None],
        (lax.axis_index("z") % 2)[None],
        core_here,
        gbar.reshape(row_blocks, rows * col_blocks, cols),
        *[b.reshape(n_core, n_z // 4, 2, col_blocks, part, width) for b in both],
        scratch=[pltpu.VMEM((col_blocks, n_z // 2, 2, n_core * part, width), F32)],
        scalars=3,
        cost=pl.CostEstimate(flops=int(1.6e9), bytes_accessed=4 << 20, transcendentals=0),
    )
    got = lax.all_to_all(sent, "col", 0, 0, tiled=True)
    total, halves = call(
        owned_kernel,
        [(row_blocks * share, width), (n_core, row_blocks * part, width)],
        source,
        got,
        adjoint,
        scalars=1,
    )
    corner = call(
        functools.partial(corner_kernel, part),
        (n_near, count, width),
        core_here,
        lax.all_gather(halves, "core", axis=0),
        total,
        scratch=[pltpu.VMEM((row_blocks * share, width), F32)],
        scalars=1,
    )
    slices = lax.all_to_all(corner, near, 0, 0, tiled=True)
    folded, factor = lax.optimization_barrier(
        (call(fold_kernel, (n_z, count, width), slices), factor)
    )
    lines = [[(z + n_z // 2) % n_z * n_core + core for z in range(n_z)] for core in range(n_core)]
    piece = lax.all_to_all(folded, ("z", "core"), 0, 0, tiled=True, axis_index_groups=lines)
    inverse, known = call(
        invert_kernel,
        [(width, width), (width, width)],
        factor,
        factor_adj,
        cost=pl.CostEstimate(flops=int(3.2e9), bytes_accessed=1 << 19, transcendentals=0),
    )
    stage = call(
        slice_kernel,
        (n_near, count, width),
        ((core_at * n_col + col_at) * count)[None],
        piece,
        known,
        inverse,
        scalars=1,
    )
    total, stage = lax.optimization_barrier((total, stage))
    lower = call(
        lower_kernel,
        (row_blocks * share, width),
        total,
        inverse,
        cost=pl.CostEstimate(flops=int(1e8), bytes_accessed=1 << 19, transcendentals=0),
    )
    stage = lax.all_to_all(stage, near, 0, 0, tiled=True).reshape(width, width)
    corner_adj = call(finish_kernel, (width, width), stage, inverse)
    return lower.reshape(row_blocks, share, width), corner_adj


def solution(mesh):
    devices = mesh.devices
    wide = Mesh(devices.reshape(devices.shape[0] // 2, 2, devices.shape[1]), ("z", "core", "col"))
    row = ("z", "core")
    return jax.shard_map(
        per_device,
        mesh=wide,
        in_specs=(
            P(None, row, None, "col"),
            P(None, ("col",) + row, None),
            P(None, row + ("col",), None),
            P(),
            P(),
        ),
        out_specs=(P(None, row + ("col",), None), P()),
        check_vma=False,
    )
```

```python
import functools

import jax
import jax.numpy as jnp
from jax import lax
from jax.experimental import pallas as pl
from jax.experimental.pallas import tpu as pltpu
from jax.sharding import Mesh
from jax.sharding import PartitionSpec as P

HIGHEST = lax.Precision.HIGHEST
F32 = jnp.float32


def dot(a, b):
    return jnp.dot(a, b, precision=HIGHEST, preferred_element_type=F32)


def dot_tn(a, b):
    return lax.dot_general(
        a, b, (((0,), (0,)), ((), ())), precision=HIGHEST, preferred_element_type=F32
    )


def call(kernel, outs, *args, scratch=(), scalars=0, cost=None):
    specs = [pl.BlockSpec(memory_space=pltpu.SMEM)] * scalars
    specs += [pl.BlockSpec(memory_space=pltpu.VMEM)] * (len(args) - scalars)
    return pl.pallas_call(
        kernel,
        out_shape=jax.tree.map(lambda s: jax.ShapeDtypeStruct(s, F32), outs, is_leaf=lambda s: isinstance(s, tuple) and isinstance(s[0], int)),
        in_specs=specs,
        scratch_shapes=scratch,
        cost_estimate=cost,
        compiler_params=pltpu.CompilerParams(vmem_limit_bytes=32 << 20),
    )(*args)


def invert_kernel(factor_ref, adjoint_ref, out_ref, known_ref):
    n = factor_ref.shape[0] // 2
    i = lax.broadcasted_iota(jnp.int32, (n, n), 0)
    j = lax.broadcasted_iota(jnp.int32, (n, n), 1)
    lowers = [factor_ref[:n, :n], factor_ref[n:, n:]]
    now = []
    for lower in lowers:
        diagonal = jnp.where(i == j, 1.0 / jnp.where(i == j, lower, 1.0), 0.0)
        scaled = jnp.sum(diagonal, axis=1, keepdims=True) * lower * jnp.sum(diagonal, axis=0, keepdims=True)
        now.append(diagonal - jnp.where((i == j + 1) & (j % 2 == 0), scaled, 0.0))
    size = 2
    while size < n:
        below = (i // size == j // size + 1) & (j // size % 2 == 0)
        turned = [dot(x, jnp.where(below, lower, 0.0)) for x, lower in zip(now, lowers)]
        now = [x - dot(t, x) for x, t in zip(now, turned)]
        size *= 2
    out_ref[:n, :n] = now[0]
    out_ref[:n, n:] = jnp.zeros((n, n), F32)
    out_ref[n:, n:] = now[1]
    out_ref[n:, :n] = -dot(dot(now[1], factor_ref[n:, :n]), now[0])
    known_ref[...] = dot_tn(adjoint_ref[...], factor_ref[...])


def product_kernel(parity_ref, turn_ref, core_ref, gbar_ref, first_ref, second_ref, out_ref, column_ref):
    n_core, pairs, _, _, part, width = first_ref.shape
    col_blocks = column_ref.shape[0]
    row_blocks = gbar_ref.shape[0]
    cols = gbar_ref.shape[2]
    rows = gbar_ref.shape[1] // col_blocks
    share = rows // out_ref.shape[0]
    n_col = out_ref.shape[0]
    for c in range(col_blocks):
        for flip in range(2):
            for core in range(n_core):
                for at, from_ref in ((0, first_ref), (pairs, second_ref)):
                    held = from_ref[turn_ref[0] ^ (flip ^ core), :, flip, c]
                    column_ref[c, at:at + pairs, flip, core * part:(core + 1) * part, :] = held
    full = column_ref[...].reshape(col_blocks * cols, width)
    for b in range(row_blocks):
        left = jnp.concatenate(
            [gbar_ref[b, pl.ds(c, rows, stride=col_blocks), :] for c in range(col_blocks)], axis=1
        )
        out_ref[:, b * share:(b + 1) * share, :] = dot(left, full).reshape(n_col, share, width)
    ratio = col_blocks // row_blocks
    for b in range(row_blocks):
        local = column_ref[b * ratio + parity_ref[0]].reshape(n_col, share, width)
        at = row_blocks * share + b * part
        out_ref[:, at:at + part, :] = jnp.where(core_ref[0] == 0, local[:, :part], local[:, part:])


def owned_kernel(source_ref, got_ref, adjoint_ref, total_ref, halves_ref):
    owned = adjoint_ref.shape[0]
    total_ref[...] = adjoint_ref[...] - 2.0 * jnp.sum(got_ref[:, :owned, :], axis=0)
    for core in range(halves_ref.shape[0]):
        halves_ref[core] = got_ref[source_ref[0] + core, owned:, :]


def corner_kernel(part, core_ref, halves_ref, total_ref, corner_ref, mine_ref):
    n_core, _, half, _ = halves_ref.shape
    for core in range(n_core):
        rows = halves_ref[core, core_ref[0]]
        for b in range(half // part):
            at = (b * n_core + core) * part
            mine_ref[at:at + part, :] = rows[b * part:(b + 1) * part]
    corner_ref[...] = dot_tn(mine_ref[...], total_ref[...]).reshape(corner_ref.shape)


def lower_kernel(total_ref, inverse_ref, out_ref):
    out_ref[...] = dot(total_ref[...], inverse_ref[...])


def fold_kernel(parts_ref, out_ref):
    total = jnp.sum(parts_ref[...], axis=0)
    out_ref[...] = jnp.broadcast_to(total[None], out_ref.shape)


def slice_kernel(begin_ref, parts_ref, known_ref, inverse_ref, out_ref):
    count = out_ref.shape[1]
    begin = pl.multiple_of(begin_ref[0], count)
    projected = known_ref[pl.ds(begin, count), :] - jnp.sum(parts_ref[...], axis=0)
    at_row = begin + lax.broadcasted_iota(jnp.int32, projected.shape, 0)
    at_col = lax.broadcasted_iota(jnp.int32, projected.shape, 1)
    halved = jnp.where(at_row < at_col, projected, jnp.where(at_row == at_col, 0.5 * projected, 0.0))
    stage = dot(halved, inverse_ref[...])
    out_ref[...] = jnp.broadcast_to(stage[None], out_ref.shape)


def finish_kernel(stage_ref, inverse_ref, out_ref):
    middle = dot_tn(inverse_ref[...], stage_ref[...])
    out_ref[...] = 0.5 * (middle + middle.T)


def per_device(gbar, panel, panel_adj, factor, factor_adj):
    n_z, n_core, n_col = (lax.axis_size(a) for a in ("z", "core", "col"))
    core_at = lax.axis_index("core")
    col_at = lax.axis_index("col")
    row_at = lax.axis_index("z") * n_core + core_at
    width = factor.shape[0]
    row_blocks, rows, col_blocks, cols = gbar.shape
    share = panel_adj.shape[1]
    part = panel.shape[1]
    near = ("core", "col")
    n_near = n_core * n_col
    count = width // n_near
    rings = [[2 * z + (z + start) % 2 for z in range(n_z)] for start in range(2)]
    along_z = lax.all_gather(panel, ("z", "core"), axis=0, axis_index_groups=rings, tiled=True)
    middle = n_z * col_blocks // 2
    first = lax.all_gather(along_z[:middle], "core", axis=0, tiled=True)
    rest, first = lax.optimization_barrier((along_z[middle:], first))
    both = [first, lax.all_gather(rest, "core", axis=0, tiled=True)]
    source = (lax.axis_index("z") * n_core % n_col)[None]
    core_here = core_at[None]
    adjoint = panel_adj.reshape(row_blocks * share, width)
    *both, source, core_here, adjoint = lax.optimization_barrier((*both, source, core_here, adjoint))
    sent = call(
        product_kernel,
        (n_col, row_blocks * (share + part), width),
        (row_at // n_col)[None],
        (lax.axis_index("z") % 2)[None],
        core_here,
        gbar.reshape(row_blocks, rows * col_blocks, cols),
        *[b.reshape(n_core, n_z // 4, 2, col_blocks, part, width) for b in both],
        scratch=[pltpu.VMEM((col_blocks, n_z // 2, 2, n_core * part, width), F32)],
        scalars=3,
        cost=pl.CostEstimate(flops=int(1.6e9), bytes_accessed=4 << 20, transcendentals=0),
    )
    got = lax.all_to_all(sent, "col", 0, 0, tiled=True)
    total, halves = call(
        owned_kernel,
        [(row_blocks * share, width), (n_core, row_blocks * part, width)],
        source,
        got,
        adjoint,
        scalars=1,
    )
    corner = call(
        functools.partial(corner_kernel, part),
        (n_near, count, width),
        core_here,
        lax.all_gather(halves, "core", axis=0),
        total,
        scratch=[pltpu.VMEM((row_blocks * share, width), F32)],
        scalars=1,
    )
    slices = lax.all_to_all(corner, near, 0, 0, tiled=True)
    folded, factor = lax.optimization_barrier(
        (call(fold_kernel, (n_z, count, width), slices), factor)
    )
    lines = [[(z + n_z // 2) % n_z * n_core + core for z in range(n_z)] for core in range(n_core)]
    piece = lax.all_to_all(folded, ("z", "core"), 0, 0, tiled=True, axis_index_groups=lines)
    inverse, known = call(
        invert_kernel,
        [(width, width), (width, width)],
        factor,
        factor_adj,
        cost=pl.CostEstimate(flops=int(3.2e9), bytes_accessed=1 << 19, transcendentals=0),
    )
    lower = call(
        lower_kernel,
        (row_blocks * share, width),
        total,
        inverse,
        cost=pl.CostEstimate(flops=int(1e8), bytes_accessed=1 << 19, transcendentals=0),
    )
    known, lower = lax.optimization_barrier((known, lower))
    stage = call(
        slice_kernel,
        (n_near, count, width),
        ((core_at * n_col + col_at) * count)[None],
        piece,
        known,
        inverse,
        scalars=1,
    )
    stage = lax.all_to_all(stage, near, 0, 0, tiled=True).reshape(width, width)
    corner_adj = call(finish_kernel, (width, width), stage, inverse)
    return lower.reshape(row_blocks, share, width), corner_adj


def solution(mesh):
    devices = mesh.devices
    wide = Mesh(devices.reshape(devices.shape[0] // 2, 2, devices.shape[1]), ("z", "core", "col"))
    row = ("z", "core")
    return jax.shard_map(
        per_device,
        mesh=wide,
        in_specs=(
            P(None, row, None, "col"),
            P(None, ("col",) + row, None),
            P(None, row + ("col",), None),
            P(),
            P(),
        ),
        out_specs=(P(None, row + ("col",), None), P()),
        check_vma=False,
    )
```

```python
import functools

import jax
import jax.numpy as jnp
from jax import lax
from jax.experimental import pallas as pl
from jax.experimental.pallas import tpu as pltpu
from jax.sharding import Mesh
from jax.sharding import PartitionSpec as P

HIGHEST = lax.Precision.HIGHEST
F32 = jnp.float32


def dot(a, b):
    return jnp.dot(a, b, precision=HIGHEST, preferred_element_type=F32)


def dot_tn(a, b):
    return lax.dot_general(
        a, b, (((0,), (0,)), ((), ())), precision=HIGHEST, preferred_element_type=F32
    )


def call(kernel, outs, *args, scratch=(), scalars=0, cost=None):
    specs = [pl.BlockSpec(memory_space=pltpu.SMEM)] * scalars
    specs += [pl.BlockSpec(memory_space=pltpu.VMEM)] * (len(args) - scalars)
    return pl.pallas_call(
        kernel,
        out_shape=jax.tree.map(lambda s: jax.ShapeDtypeStruct(s, F32), outs, is_leaf=lambda s: isinstance(s, tuple) and isinstance(s[0], int)),
        in_specs=specs,
        scratch_shapes=scratch,
        cost_estimate=cost,
        compiler_params=pltpu.CompilerParams(vmem_limit_bytes=32 << 20),
    )(*args)


def invert_kernel(factor_ref, adjoint_ref, out_ref, flipped_ref, known_ref):
    n = factor_ref.shape[0] // 2
    i = lax.broadcasted_iota(jnp.int32, (n, n), 0)
    j = lax.broadcasted_iota(jnp.int32, (n, n), 1)
    lowers = [factor_ref[:n, :n], factor_ref[n:, n:]]
    now = []
    for lower in lowers:
        diagonal = jnp.where(i == j, 1.0 / jnp.where(i == j, lower, 1.0), 0.0)
        scaled = jnp.sum(diagonal, axis=1, keepdims=True) * lower * jnp.sum(diagonal, axis=0, keepdims=True)
        now.append(diagonal - jnp.where((i == j + 1) & (j % 2 == 0), scaled, 0.0))
    size = 2
    while size < n:
        below = (i // size == j // size + 1) & (j // size % 2 == 0)
        turned = [dot(x, jnp.where(below, lower, 0.0)) for x, lower in zip(now, lowers)]
        now = [x - dot(t, x) for x, t in zip(now, turned)]
        size *= 2
    out_ref[:n, :n] = now[0]
    out_ref[:n, n:] = jnp.zeros((n, n), F32)
    out_ref[n:, n:] = now[1]
    out_ref[n:, :n] = -dot(dot(now[1], factor_ref[n:, :n]), now[0])
    flipped_ref[...] = out_ref[...].T
    known_ref[...] = dot_tn(adjoint_ref[...], factor_ref[...])


def product_kernel(parity_ref, turn_ref, core_ref, gbar_ref, first_ref, second_ref, out_ref, column_ref):
    n_core, pairs, _, _, part, width = first_ref.shape
    col_blocks = column_ref.shape[0]
    row_blocks = gbar_ref.shape[0]
    cols = gbar_ref.shape[2]
    rows = gbar_ref.shape[1] // col_blocks
    share = rows // out_ref.shape[0]
    n_col = out_ref.shape[0]
    for c in range(col_blocks):
        for flip in range(2):
            for core in range(n_core):
                for at, from_ref in ((0, first_ref), (pairs, second_ref)):
                    held = from_ref[turn_ref[0] ^ (flip ^ core), :, flip, c]
                    column_ref[c, at:at + pairs, flip, core * part:(core + 1) * part, :] = held
    full = column_ref[...].reshape(col_blocks * cols, width)
    for b in range(row_blocks):
        left = jnp.concatenate(
            [gbar_ref[b, pl.ds(c, rows, stride=col_blocks), :] for c in range(col_blocks)], axis=1
        )
        out_ref[:, b * share:(b + 1) * share, :] = dot(left, full).reshape(n_col, share, width)
    ratio = col_blocks // row_blocks
    for b in range(row_blocks):
        local = column_ref[b * ratio + parity_ref[0]].reshape(n_col, share, width)
        at = row_blocks * share + b * part
        out_ref[:, at:at + part, :] = jnp.where(core_ref[0] == 0, local[:, :part], local[:, part:])


def owned_kernel(source_ref, got_ref, adjoint_ref, total_ref, halves_ref):
    owned = adjoint_ref.shape[0]
    total_ref[...] = adjoint_ref[...] - 2.0 * jnp.sum(got_ref[:, :owned, :], axis=0)
    for core in range(halves_ref.shape[0]):
        halves_ref[core] = got_ref[source_ref[0] + core, owned:, :]


def corner_kernel(part, core_ref, halves_ref, total_ref, corner_ref, mine_ref):
    n_core, _, half, _ = halves_ref.shape
    for core in range(n_core):
        rows = halves_ref[core, core_ref[0]]
        for b in range(half // part):
            at = (b * n_core + core) * part
            mine_ref[at:at + part, :] = rows[b * part:(b + 1) * part]
    corner_ref[...] = dot_tn(mine_ref[...], total_ref[...]).reshape(corner_ref.shape)


def lower_kernel(total_ref, inverse_ref, out_ref):
    out_ref[...] = dot(total_ref[...], inverse_ref[...])


def fold_kernel(parts_ref, out_ref):
    total = jnp.sum(parts_ref[...], axis=0)
    out_ref[...] = jnp.broadcast_to(total[None], out_ref.shape)


def slice_kernel(begin_ref, parts_ref, known_ref, inverse_ref, out_ref):
    count = out_ref.shape[1]
    begin = pl.multiple_of(begin_ref[0], count)
    projected = known_ref[pl.ds(begin, count), :] - jnp.sum(parts_ref[...], axis=0)
    at_row = begin + lax.broadcasted_iota(jnp.int32, projected.shape, 0)
    at_col = lax.broadcasted_iota(jnp.int32, projected.shape, 1)
    halved = jnp.where(at_row < at_col, projected, jnp.where(at_row == at_col, 0.5 * projected, 0.0))
    stage = dot(halved, inverse_ref[...])
    out_ref[...] = jnp.broadcast_to(stage[None], out_ref.shape)


def finish_kernel(stage_ref, flipped_ref, out_ref):
    middle = dot(flipped_ref[...], stage_ref[...])
    out_ref[...] = 0.5 * (middle + middle.T)


def per_device(gbar, panel, panel_adj, factor, factor_adj):
    n_z, n_core, n_col = (lax.axis_size(a) for a in ("z", "core", "col"))
    core_at = lax.axis_index("core")
    col_at = lax.axis_index("col")
    row_at = lax.axis_index("z") * n_core + core_at
    width = factor.shape[0]
    row_blocks, rows, col_blocks, cols = gbar.shape
    share = panel_adj.shape[1]
    part = panel.shape[1]
    near = ("core", "col")
    n_near = n_core * n_col
    count = width // n_near
    rings = [[2 * z + (z + start) % 2 for z in range(n_z)] for start in range(2)]
    along_z = lax.all_gather(panel, ("z", "core"), axis=0, axis_index_groups=rings, tiled=True)
    middle = n_z * col_blocks // 2
    first = lax.all_gather(along_z[:middle], "core", axis=0, tiled=True)
    rest, first = lax.optimization_barrier((along_z[middle:], first))
    both = [first, lax.all_gather(rest, "core", axis=0, tiled=True)]
    source = (lax.axis_index("z") * n_core % n_col)[None]
    core_here = core_at[None]
    adjoint = panel_adj.reshape(row_blocks * share, width)
    *both, source, core_here, adjoint = lax.optimization_barrier((*both, source, core_here, adjoint))
    sent = call(
        product_kernel,
        (n_col, row_blocks * (share + part), width),
        (row_at // n_col)[None],
        (lax.axis_index("z") % 2)[None],
        core_here,
        gbar.reshape(row_blocks, rows * col_blocks, cols),
        *[b.reshape(n_core, n_z // 4, 2, col_blocks, part, width) for b in both],
        scratch=[pltpu.VMEM((col_blocks, n_z // 2, 2, n_core * part, width), F32)],
        scalars=3,
        cost=pl.CostEstimate(flops=int(1.6e9), bytes_accessed=4 << 20, transcendentals=0),
    )
    got = lax.all_to_all(sent, "col", 0, 0, tiled=True)
    total, halves = call(
        owned_kernel,
        [(row_blocks * share, width), (n_core, row_blocks * part, width)],
        source,
        got,
        adjoint,
        scalars=1,
    )
    corner = call(
        functools.partial(corner_kernel, part),
        (n_near, count, width),
        core_here,
        lax.all_gather(halves, "core", axis=0),
        total,
        scratch=[pltpu.VMEM((row_blocks * share, width), F32)],
        scalars=1,
    )
    slices = lax.all_to_all(corner, near, 0, 0, tiled=True)
    folded, factor = lax.optimization_barrier(
        (call(fold_kernel, (n_z, count, width), slices), factor)
    )
    lines = [[(z + n_z // 2) % n_z * n_core + core for z in range(n_z)] for core in range(n_core)]
    piece = lax.all_to_all(folded, ("z", "core"), 0, 0, tiled=True, axis_index_groups=lines)
    inverse, flipped, known = call(
        invert_kernel,
        [(width, width)] * 3,
        factor,
        factor_adj,
        cost=pl.CostEstimate(flops=int(3.2e9), bytes_accessed=1 << 19, transcendentals=0),
    )
    lower = call(
        lower_kernel,
        (row_blocks * share, width),
        total,
        inverse,
        cost=pl.CostEstimate(flops=int(1e8), bytes_accessed=1 << 19, transcendentals=0),
    )
    known, lower = lax.optimization_barrier((known, lower))
    stage = call(
        slice_kernel,
        (n_col, count, width),
        ((core_at * n_col + col_at) * count)[None],
        piece,
        known,
        inverse,
        scalars=1,
    )
    stage = lax.all_to_all(stage, "col", 0, 0, tiled=True)
    stage = lax.all_gather(stage, "core", axis=0).reshape(width, width)
    corner_adj = call(finish_kernel, (width, width), stage, flipped)
    return lower.reshape(row_blocks, share, width), corner_adj


def solution(mesh):
    devices = mesh.devices
    wide = Mesh(devices.reshape(devices.shape[0] // 2, 2, devices.shape[1]), ("z", "core", "col"))
    row = ("z", "core")
    return jax.shard_map(
        per_device,
        mesh=wide,
        in_specs=(
            P(None, row, None, "col"),
            P(None, ("col",) + row, None),
            P(None, row + ("col",), None),
            P(),
            P(),
        ),
        out_specs=(P(None, row + ("col",), None), P()),
        check_vma=False,
    )
```

```python
import functools

import jax
import jax.numpy as jnp
from jax import lax
from jax.experimental import pallas as pl
from jax.experimental.pallas import tpu as pltpu
from jax.sharding import Mesh
from jax.sharding import PartitionSpec as P

HIGHEST = lax.Precision.HIGHEST
F32 = jnp.float32


def dot(a, b):
    return jnp.dot(a, b, precision=HIGHEST, preferred_element_type=F32)


def dot_tn(a, b):
    return lax.dot_general(
        a, b, (((0,), (0,)), ((), ())), precision=HIGHEST, preferred_element_type=F32
    )


def call(kernel, outs, *args, scratch=(), scalars=0, cost=None):
    specs = [pl.BlockSpec(memory_space=pltpu.SMEM)] * scalars
    specs += [pl.BlockSpec(memory_space=pltpu.VMEM)] * (len(args) - scalars)
    return pl.pallas_call(
        kernel,
        out_shape=jax.tree.map(lambda s: jax.ShapeDtypeStruct(s, F32), outs, is_leaf=lambda s: isinstance(s, tuple) and isinstance(s[0], int)),
        in_specs=specs,
        scratch_shapes=scratch,
        cost_estimate=cost,
        compiler_params=pltpu.CompilerParams(vmem_limit_bytes=32 << 20),
    )(*args)


def invert_kernel(factor_ref, adjoint_ref, out_ref, known_ref):
    n = factor_ref.shape[0] // 2
    i = lax.broadcasted_iota(jnp.int32, (n, n), 0)
    j = lax.broadcasted_iota(jnp.int32, (n, n), 1)
    lowers = [factor_ref[:n, :n], factor_ref[n:, n:]]
    now = []
    for lower in lowers:
        diagonal = jnp.where(i == j, 1.0 / jnp.where(i == j, lower, 1.0), 0.0)
        scaled = jnp.sum(diagonal, axis=1, keepdims=True) * lower * jnp.sum(diagonal, axis=0, keepdims=True)
        now.append(diagonal - jnp.where((i == j + 1) & (j % 2 == 0), scaled, 0.0))
    size = 2
    while size < n:
        below = (i // size == j // size + 1) & (j // size % 2 == 0)
        turned = [dot(x, jnp.where(below, lower, 0.0)) for x, lower in zip(now, lowers)]
        now = [x - dot(t, x) for x, t in zip(now, turned)]
        size *= 2
    out_ref[:n, :n] = now[0]
    out_ref[:n, n:] = jnp.zeros((n, n), F32)
    out_ref[n:, n:] = now[1]
    out_ref[n:, :n] = -dot(dot(now[1], factor_ref[n:, :n]), now[0])
    known_ref[...] = dot_tn(adjoint_ref[...], factor_ref[...])


def product_kernel(parity_ref, turn_ref, core_ref, gbar_ref, first_ref, second_ref, out_ref, column_ref):
    n_core, pairs, _, _, part, width = first_ref.shape
    col_blocks = column_ref.shape[0]
    row_blocks = gbar_ref.shape[0]
    cols = gbar_ref.shape[2]
    rows = gbar_ref.shape[1] // col_blocks
    share = rows // out_ref.shape[0]
    n_col = out_ref.shape[0]
    for c in range(col_blocks):
        for flip in range(2):
            for core in range(n_core):
                for at, from_ref in ((0, first_ref), (pairs, second_ref)):
                    held = from_ref[turn_ref[0] ^ (flip ^ core), :, flip, c]
                    column_ref[c, at:at + pairs, flip, core * part:(core + 1) * part, :] = held
    full = column_ref[...].reshape(col_blocks * cols, width)
    left = jnp.concatenate(
        [gbar_ref[:, pl.ds(c, rows, stride=col_blocks), :] for c in range(col_blocks)], axis=2
    )
    product = dot(left.reshape(row_blocks * rows, col_blocks * cols), full)
    for b in range(row_blocks):
        block = product[b * rows:(b + 1) * rows]
        out_ref[:, b * share:(b + 1) * share, :] = block.reshape(n_col, share, width)
    ratio = col_blocks // row_blocks
    for b in range(row_blocks):
        local = column_ref[b * ratio + parity_ref[0]].reshape(n_col, share, width)
        at = row_blocks * share + b * part
        out_ref[:, at:at + part, :] = jnp.where(core_ref[0] == 0, local[:, :part], local[:, part:])


def owned_kernel(source_ref, got_ref, adjoint_ref, total_ref, halves_ref):
    owned = adjoint_ref.shape[0]
    total_ref[...] = adjoint_ref[...] - 2.0 * jnp.sum(got_ref[:, :owned, :], axis=0)
    for core in range(halves_ref.shape[0]):
        halves_ref[core] = got_ref[source_ref[0] + core, owned:, :]


def corner_kernel(part, core_ref, halves_ref, total_ref, corner_ref, mine_ref):
    n_core, _, half, _ = halves_ref.shape
    for core in range(n_core):
        rows = halves_ref[core, core_ref[0]]
        for b in range(half // part):
            at = (b * n_core + core) * part
            mine_ref[at:at + part, :] = rows[b * part:(b + 1) * part]
    corner_ref[...] = dot_tn(mine_ref[...], total_ref[...]).reshape(corner_ref.shape)


def lower_kernel(total_ref, inverse_ref, out_ref):
    out_ref[...] = dot(total_ref[...], inverse_ref[...])


def fold_kernel(parts_ref, out_ref):
    total = jnp.sum(parts_ref[...], axis=0)
    out_ref[...] = jnp.broadcast_to(total[None], out_ref.shape)


def slice_kernel(begin_ref, parts_ref, known_ref, inverse_ref, out_ref):
    count = out_ref.shape[1]
    begin = pl.multiple_of(begin_ref[0], count)
    projected = known_ref[pl.ds(begin, count), :] - jnp.sum(parts_ref[...], axis=0)
    at_row = begin + lax.broadcasted_iota(jnp.int32, projected.shape, 0)
    at_col = lax.broadcasted_iota(jnp.int32, projected.shape, 1)
    halved = jnp.where(at_row < at_col, projected, jnp.where(at_row == at_col, 0.5 * projected, 0.0))
    stage = dot(halved, inverse_ref[...])
    out_ref[...] = jnp.broadcast_to(stage[None], out_ref.shape)


def finish_kernel(stage_ref, inverse_ref, out_ref):
    middle = dot_tn(inverse_ref[...], stage_ref[...])
    out_ref[...] = 0.5 * (middle + middle.T)


def per_device(gbar, panel, panel_adj, factor, factor_adj):
    n_z, n_core, n_col = (lax.axis_size(a) for a in ("z", "core", "col"))
    core_at = lax.axis_index("core")
    col_at = lax.axis_index("col")
    row_at = lax.axis_index("z") * n_core + core_at
    width = factor.shape[0]
    row_blocks, rows, col_blocks, cols = gbar.shape
    share = panel_adj.shape[1]
    part = panel.shape[1]
    near = ("core", "col")
    n_near = n_core * n_col
    count = width // n_near
    rings = [[2 * z + (z + start) % 2 for z in range(n_z)] for start in range(2)]
    along_z = lax.all_gather(panel, ("z", "core"), axis=0, axis_index_groups=rings, tiled=True)
    middle = n_z * col_blocks // 2
    first = lax.all_gather(along_z[:middle], "core", axis=0, tiled=True)
    rest, first = lax.optimization_barrier((along_z[middle:], first))
    both = [first, lax.all_gather(rest, "core", axis=0, tiled=True)]
    source = (lax.axis_index("z") * n_core % n_col)[None]
    core_here = core_at[None]
    adjoint = panel_adj.reshape(row_blocks * share, width)
    *both, source, core_here, adjoint = lax.optimization_barrier((*both, source, core_here, adjoint))
    sent = call(
        product_kernel,
        (n_col, row_blocks * (share + part), width),
        (row_at // n_col)[None],
        (lax.axis_index("z") % 2)[None],
        core_here,
        gbar.reshape(row_blocks, rows * col_blocks, cols),
        *[b.reshape(n_core, n_z // 4, 2, col_blocks, part, width) for b in both],
        scratch=[pltpu.VMEM((col_blocks, n_z // 2, 2, n_core * part, width), F32)],
        scalars=3,
        cost=pl.CostEstimate(flops=int(1.6e9), bytes_accessed=4 << 20, transcendentals=0),
    )
    got = lax.all_to_all(sent, "col", 0, 0, tiled=True)
    total, halves = call(
        owned_kernel,
        [(row_blocks * share, width), (n_core, row_blocks * part, width)],
        source,
        got,
        adjoint,
        scalars=1,
    )
    corner = call(
        functools.partial(corner_kernel, part),
        (n_near, count, width),
        core_here,
        lax.all_gather(halves, "core", axis=0),
        total,
        scratch=[pltpu.VMEM((row_blocks * share, width), F32)],
        scalars=1,
    )
    slices = lax.all_to_all(corner, near, 0, 0, tiled=True)
    folded, factor = lax.optimization_barrier(
        (call(fold_kernel, (n_z, count, width), slices), factor)
    )
    lines = [[(z + n_z // 2) % n_z * n_core + core for z in range(n_z)] for core in range(n_core)]
    piece = lax.all_to_all(folded, ("z", "core"), 0, 0, tiled=True, axis_index_groups=lines)
    inverse, known = call(
        invert_kernel,
        [(width, width), (width, width)],
        factor,
        factor_adj,
        cost=pl.CostEstimate(flops=int(3.2e9), bytes_accessed=1 << 19, transcendentals=0),
    )
    lower = call(
        lower_kernel,
        (row_blocks * share, width),
        total,
        inverse,
        cost=pl.CostEstimate(flops=int(1e8), bytes_accessed=1 << 19, transcendentals=0),
    )
    known, lower = lax.optimization_barrier((known, lower))
    stage = call(
        slice_kernel,
        (n_near, count, width),
        ((core_at * n_col + col_at) * count)[None],
        piece,
        known,
        inverse,
        scalars=1,
    )
    stage = lax.all_to_all(stage, near, 0, 0, tiled=True).reshape(width, width)
    corner_adj = call(finish_kernel, (width, width), stage, inverse)
    return lower.reshape(row_blocks, share, width), corner_adj


def solution(mesh):
    devices = mesh.devices
    wide = Mesh(devices.reshape(devices.shape[0] // 2, 2, devices.shape[1]), ("z", "core", "col"))
    row = ("z", "core")
    return jax.shard_map(
        per_device,
        mesh=wide,
        in_specs=(
            P(None, row, None, "col"),
            P(None, ("col",) + row, None),
            P(None, row + ("col",), None),
            P(),
            P(),
        ),
        out_specs=(P(None, row + ("col",), None), P()),
        check_vma=False,
    )
```

```python
import functools

import jax
import jax.numpy as jnp
from jax import lax
from jax.experimental import pallas as pl
from jax.experimental.pallas import tpu as pltpu
from jax.sharding import Mesh
from jax.sharding import PartitionSpec as P

HIGHEST = lax.Precision.HIGHEST
F32 = jnp.float32


def dot(a, b):
    return jnp.dot(a, b, precision=HIGHEST, preferred_element_type=F32)


def dot_tn(a, b):
    return lax.dot_general(
        a, b, (((0,), (0,)), ((), ())), precision=HIGHEST, preferred_element_type=F32
    )


def call(kernel, outs, *args, scratch=(), scalars=0, cost=None):
    specs = [pl.BlockSpec(memory_space=pltpu.SMEM)] * scalars
    specs += [pl.BlockSpec(memory_space=pltpu.VMEM)] * (len(args) - scalars)
    return pl.pallas_call(
        kernel,
        out_shape=jax.tree.map(lambda s: jax.ShapeDtypeStruct(s, F32), outs, is_leaf=lambda s: isinstance(s, tuple) and isinstance(s[0], int)),
        in_specs=specs,
        scratch_shapes=scratch,
        cost_estimate=cost,
        compiler_params=pltpu.CompilerParams(vmem_limit_bytes=32 << 20),
    )(*args)


def invert_kernel(factor_ref, adjoint_ref, out_ref, known_ref):
    n = factor_ref.shape[0] // 2
    i = lax.broadcasted_iota(jnp.int32, (n, n), 0)
    j = lax.broadcasted_iota(jnp.int32, (n, n), 1)
    lowers = [factor_ref[:n, :n], factor_ref[n:, n:]]
    now = []
    for lower in lowers:
        diagonal = jnp.where(i == j, 1.0 / jnp.where(i == j, lower, 1.0), 0.0)
        scaled = jnp.sum(diagonal, axis=1, keepdims=True) * lower * jnp.sum(diagonal, axis=0, keepdims=True)
        now.append(diagonal - jnp.where((i == j + 1) & (j % 2 == 0), scaled, 0.0))
    size = 2
    while size < n:
        below = (i // size == j // size + 1) & (j // size % 2 == 0)
        turned = [dot(x, jnp.where(below, lower, 0.0)) for x, lower in zip(now, lowers)]
        now = [x - dot(t, x) for x, t in zip(now, turned)]
        size *= 2
    out_ref[:n, :n] = now[0]
    out_ref[:n, n:] = jnp.zeros((n, n), F32)
    out_ref[n:, n:] = now[1]
    out_ref[n:, :n] = -dot(dot(now[1], factor_ref[n:, :n]), now[0])
    known_ref[...] = dot_tn(adjoint_ref[...], factor_ref[...])


def product_kernel(parity_ref, turn_ref, core_ref, gbar_ref, first_ref, second_ref, out_ref, column_ref):
    n_core, pairs, _, _, part, width = first_ref.shape
    col_blocks = column_ref.shape[0]
    row_blocks = gbar_ref.shape[0]
    cols = gbar_ref.shape[2]
    rows = gbar_ref.shape[1] // col_blocks
    share = rows // out_ref.shape[0]
    n_col = out_ref.shape[0]
    for c in range(col_blocks):
        for flip in range(2):
            for core in range(n_core):
                for at, from_ref in ((0, first_ref), (pairs, second_ref)):
                    held = from_ref[turn_ref[0] ^ (flip ^ core), :, flip, c]
                    column_ref[c, at:at + pairs, flip, core * part:(core + 1) * part, :] = held
    full = column_ref[...].reshape(col_blocks * cols, width)
    for b in range(row_blocks):
        left = jnp.concatenate(
            [gbar_ref[b, pl.ds(c, rows, stride=col_blocks), :] for c in range(col_blocks)], axis=1
        )
        out_ref[:, b * share:(b + 1) * share, :] = dot(left, full).reshape(n_col, share, width)
    ratio = col_blocks // row_blocks
    for b in range(row_blocks):
        local = column_ref[b * ratio + parity_ref[0]].reshape(n_col, share, width)
        at = row_blocks * share + b * part
        out_ref[:, at:at + part, :] = jnp.where(core_ref[0] == 0, local[:, :part], local[:, part:])


def owned_kernel(source_ref, got_ref, adjoint_ref, total_ref, halves_ref):
    owned = adjoint_ref.shape[0]
    total_ref[...] = adjoint_ref[...] - 2.0 * jnp.sum(got_ref[:, :owned, :], axis=0)
    for core in range(halves_ref.shape[0]):
        halves_ref[core] = got_ref[source_ref[0] + core, owned:, :]


def corner_kernel(part, core_ref, turn_ref, halves_ref, total_ref, corner_ref, mine_ref):
    n_core, _, half, _ = halves_ref.shape
    for core in range(n_core):
        rows = halves_ref[core, core_ref[0]]
        for b in range(half // part):
            at = (b * n_core + core) * part
            mine_ref[at:at + part, :] = rows[b * part:(b + 1) * part]
    corner = dot_tn(mine_ref[...], total_ref[...])
    n_col = corner_ref.shape[0] // n_core
    for core in range(n_core):
        held = corner[core * n_col * corner_ref.shape[1]:(core + 1) * n_col * corner_ref.shape[1]]
        at = (turn_ref[0] ^ core) * n_col
        corner_ref[pl.ds(at, n_col)] = held.reshape(n_col, *corner_ref.shape[1:])


def lower_kernel(total_ref, inverse_ref, out_ref):
    out_ref[...] = dot(total_ref[...], inverse_ref[...])


def fold_kernel(parts_ref, out_ref):
    total = jnp.sum(parts_ref[...], axis=0)
    out_ref[...] = jnp.broadcast_to(total[None], out_ref.shape)


def slice_kernel(begin_ref, parts_ref, known_ref, inverse_ref, out_ref):
    count = out_ref.shape[1]
    begin = pl.multiple_of(begin_ref[0], count)
    projected = known_ref[pl.ds(begin, count), :] - jnp.sum(parts_ref[...], axis=0)
    at_row = begin + lax.broadcasted_iota(jnp.int32, projected.shape, 0)
    at_col = lax.broadcasted_iota(jnp.int32, projected.shape, 1)
    halved = jnp.where(at_row < at_col, projected, jnp.where(at_row == at_col, 0.5 * projected, 0.0))
    stage = dot(halved, inverse_ref[...])
    out_ref[...] = jnp.broadcast_to(stage[None], out_ref.shape)


def finish_kernel(turn_ref, stage_ref, inverse_ref, out_ref):
    stage = jnp.concatenate([stage_ref[turn_ref[0] ^ core] for core in range(2)], axis=0)
    middle = dot_tn(inverse_ref[...], stage)
    out_ref[...] = 0.5 * (middle + middle.T)


def per_device(gbar, panel, panel_adj, factor, factor_adj):
    n_z, n_core, n_col = (lax.axis_size(a) for a in ("z", "core", "col"))
    core_at = lax.axis_index("core")
    col_at = lax.axis_index("col")
    row_at = lax.axis_index("z") * n_core + core_at
    width = factor.shape[0]
    row_blocks, rows, col_blocks, cols = gbar.shape
    share = panel_adj.shape[1]
    part = panel.shape[1]
    near = ("core", "col")
    n_near = n_core * n_col
    count = width // n_near
    rings = [[2 * z + (z + start) % 2 for z in range(n_z)] for start in range(2)]
    along_z = lax.all_gather(panel, ("z", "core"), axis=0, axis_index_groups=rings, tiled=True)
    middle = n_z * col_blocks // 2
    first = lax.all_gather(along_z[:middle], "core", axis=0, tiled=True)
    rest, first = lax.optimization_barrier((along_z[middle:], first))
    both = [first, lax.all_gather(rest, "core", axis=0, tiled=True)]
    source = (lax.axis_index("z") * n_core % n_col)[None]
    core_here = core_at[None]
    turn = (lax.axis_index("z") % 2)[None]
    adjoint = panel_adj.reshape(row_blocks * share, width)
    *both, source, core_here, turn, adjoint = lax.optimization_barrier((*both, source, core_here, turn, adjoint))
    sent = call(
        product_kernel,
        (n_col, row_blocks * (share + part), width),
        (row_at // n_col)[None],
        turn,
        core_here,
        gbar.reshape(row_blocks, rows * col_blocks, cols),
        *[b.reshape(n_core, n_z // 4, 2, col_blocks, part, width) for b in both],
        scratch=[pltpu.VMEM((col_blocks, n_z // 2, 2, n_core * part, width), F32)],
        scalars=3,
        cost=pl.CostEstimate(flops=int(1.6e9), bytes_accessed=4 << 20, transcendentals=0),
    )
    got = lax.all_to_all(sent, "col", 0, 0, tiled=True)
    total, halves = call(
        owned_kernel,
        [(row_blocks * share, width), (n_core, row_blocks * part, width)],
        source,
        got,
        adjoint,
        scalars=1,
    )
    corner = call(
        functools.partial(corner_kernel, part),
        (n_near, count, width),
        core_here,
        turn,
        lax.all_gather(halves, "core", axis=0),
        total,
        scratch=[pltpu.VMEM((row_blocks * share, width), F32)],
        scalars=2,
    )
    slices = lax.all_to_all(corner, near, 0, 0, tiled=True)
    folded, factor = lax.optimization_barrier(
        (call(fold_kernel, (n_z, count, width), slices), factor)
    )
    lines = [ring[n_z // 2:] + ring[:n_z // 2] for ring in rings]
    piece = lax.all_to_all(folded, ("z", "core"), 0, 0, tiled=True, axis_index_groups=lines)
    inverse, known = call(
        invert_kernel,
        [(width, width), (width, width)],
        factor,
        factor_adj,
        cost=pl.CostEstimate(flops=int(3.2e9), bytes_accessed=1 << 19, transcendentals=0),
    )
    lower = call(
        lower_kernel,
        (row_blocks * share, width),
        total,
        inverse,
        cost=pl.CostEstimate(flops=int(1e8), bytes_accessed=1 << 19, transcendentals=0),
    )
    known, lower = lax.optimization_barrier((known, lower))
    stage = call(
        slice_kernel,
        (n_near, count, width),
        (((core_at ^ turn[0]) * n_col + col_at) * count)[None],
        piece,
        known,
        inverse,
        scalars=1,
    )
    stage = lax.all_to_all(stage, near, 0, 0, tiled=True)
    stage = stage.reshape(n_core, width // n_core, width)
    corner_adj = call(finish_kernel, (width, width), turn, stage, inverse, scalars=1)
    return lower.reshape(row_blocks, share, width), corner_adj


def solution(mesh):
    devices = mesh.devices
    wide = Mesh(devices.reshape(devices.shape[0] // 2, 2, devices.shape[1]), ("z", "core", "col"))
    row = ("z", "core")
    return jax.shard_map(
        per_device,
        mesh=wide,
        in_specs=(
            P(None, row, None, "col"),
            P(None, ("col",) + row, None),
            P(None, row + ("col",), None),
            P(),
            P(),
        ),
        out_specs=(P(None, row + ("col",), None), P()),
        check_vma=False,
    )
```
